128 devices in a mesh: seq: 8 (over z, core), row: 4 (over y), col: 4 (over x).
Axes of the slice: x: 4, y: 4, z: 4, core: 2. Of those that a mesh axis runs over, the one named last changes fastest.
Arguments:
- tokens: bfloat16 [4096, 4096], P('seq', ('row', 'col')), may hold values from -6 to 6
- lengths: int32 [16], replicated, may hold values from 1 to 1024, 4096 in all
- deal: int32 [16], replicated, may hold values from 0 to 15, each once
- pre_gain: float32 [4096], replicated, may hold values from 0.5 to 1.5
- w_inner: bfloat16 [4096, 2, 8192], P(None, None, ('row', 'col'))
- w_group: bfloat16 [4096, 2, 8, 128], P(None, None, 'row'), may hold values from -0.09375 to 0.09375
- w_step: bfloat16 [4096, 128], P(None, ('row', 'col')), may hold values from -0.09375 to 0.09375
- conv_inner: float32 [4, 8192], P(None, ('row', 'col')), may hold values from -0.5 to 0.5
- conv_group: float32 [4, 2, 8, 128], P(None, None, 'row'), may hold values from -0.5 to 0.5
- conv_bias_inner: float32 [8192], P(('row', 'col')), may hold values from -0.5 to 0.5
- conv_bias_group: float32 [2, 8, 128], P(None, 'row'), may hold values from -0.5 to 0.5
- edge_inner: bfloat16 [16, 3, 8192], P(None, None, ('row', 'col')), may hold values from -6 to 6
- edge_group: bfloat16 [16, 3, 2, 8, 128], P(None, None, None, 'row'), may hold values from -6 to 6
- init_states: float32 [16, 128, 64, 128], P(None, ('row', 'col')), may hold values from -1.25 to 1.25
- step_bias: float32 [128], P(('row', 'col')), may hold values from -5.3 to -2.3
- decay_log: float32 [128], P(('row', 'col')), may hold values from -3.9 to 0
- skip: float32 [128], P(('row', 'col')), may hold values from 0.5 to 1.5
- inner_gain: float32 [8192], P(('row', 'col')), may hold values from 0.5 to 1.5
- w_out: bfloat16 [8192, 4096], P(('row', 'col')), may hold values from -0.09375 to 0.09375
- final_gain: float32 [4096], replicated, may hold values from 0.5 to 1.5
- w_head: bfloat16 [4096, 32768], P(None, ('seq', 'row', 'col')), may hold values from -0.09375 to 0.09375
Outputs:
- hidden_out: bfloat16 [4096, 4096], P('seq', ('row', 'col'))
- final_states: float32 [16, 128, 64, 128], P('seq', ('row', 'col'))
- logits: float32 [16, 32768], P(None, ('seq', 'row', 'col'))
The draws below stay inside these ranges and needn't reach their ends.
Inputs may be any that keep to these rules, and one draw needn't show every extreme that they name: The lengths sum to 4096 and the longest is exactly 1024. `deal`: each owner slot appears once.
All inputs are finite; a program needn't handle non-finite values.
Results may differ from the reference program's by a relative error of at most 0.012.
Values may be sent and summed in bfloat16 or wider, within the bound.
A program may use at most 128 MiB of HBM per device.

```python
import math
import jax
import jax.numpy as jnp
import numpy as np
from jax import lax

D = 4096
HEADS = 128
HEAD = 64
STATE = 128
GROUPS = 8
VOCAB = 32768
KERNEL = 4
BLOCK = 256
REQS = 16
E = 8192
TOKENS = 4096


def draw_w_inner(key, part):
    noise_key = jax.random.fold_in(key, 11)
    scale_key = jax.random.fold_in(key, 12)
    span = E // GROUPS
    place = (jnp.arange(E) % span).astype(jnp.float32) / span
    column = jnp.power(3.0, place - 0.5) * jnp.exp(jax.random.uniform(scale_key, (E,), jnp.float32, -0.5, 0.5))
    values = jnp.clip(jax.random.normal(noise_key, (D, 2, E), jnp.float32), -4.0, 4.0)
    return (values * column * D ** (-0.5)).astype(jnp.bfloat16)


def spiked(values, own_key, source, target, blocks, factor):
    def block_of(dim):
        return (jnp.arange(values.shape[dim]) // (values.shape[dim] // blocks)).reshape((-1,) + (1,) * (values.ndim - 1 - dim))

    near = jax.random.permutation(own_key, blocks)[block_of(target)]
    other_side = (block_of(target) + blocks // 2) % blocks
    return jnp.where((block_of(source) == near) | (block_of(source) == other_side), factor * values, values)


def steps_of(key, extent, cuts, smallest, high):
    gain, own = 1.0, jax.random.fold_in(key, 6)
    for dim, shards_of in cuts:
        heights = jnp.exp(jax.random.uniform(jax.random.fold_in(own, dim), (shards_of,), jnp.float32, smallest / len(cuts), high / len(cuts)))
        gain = gain * jnp.repeat(heights, extent[dim] // shards_of).reshape([-1 if axis == dim else 1 for axis in range(len(extent))])
    return gain


def split_up(amount, total, limit, slope):
    weights = [(1 << 20) // math.isqrt(grade ** slope) + 1 for grade in range(2, amount + 1)]
    spare, counts = total - limit - (amount - 1), [1] * (amount - 1)
    while spare > 0:
        movable = [i for i in range(amount - 1) if counts[i] < limit]
        whole, left = sum([weights[i] for i in movable]), spare
        for i in movable:
            more = min(limit - counts[i], max(1, left * weights[i] // whole), spare)
            counts[i] = counts[i] + more
            spare = spare - more
    return np.array([limit] + counts)


def uneven(own_key, number_of, total, limit, skew):
    if number_of == 2:
        one = jax.random.randint(own_key, (), max(1, total - limit), min(limit, total - 1) + 1)
        return jnp.stack([one, total - one])
    tallies = jnp.asarray(split_up(number_of, total, limit, skew), jnp.int32)
    couples = (number_of - 1) // 2
    source_of, taker = tallies[1:1 + 2 * couples:2], tallies[2:2 + 2 * couples:2]
    slack = jnp.minimum(source_of - 1, limit - taker)
    shifted = jax.random.randint(jax.random.fold_in(own_key, 1), (couples,), 0, 1 << 20) % (slack + 1)
    tallies = tallies.at[1:1 + 2 * couples:2].set(source_of - shifted).at[2:2 + 2 * couples:2].set(taker + shifted)
    return tallies[jax.random.permutation(jax.random.fold_in(own_key, 2), number_of)]


def scatter_about(key, extent, width, bound, shards=(), kind=jnp.bfloat16):
    level = steps_of(key, extent, shards, -0.22, 0.18) if shards else 1.0
    values = jax.random.normal(key, extent, jnp.float32) * width * level
    return jnp.minimum(jnp.maximum(values, -bound), bound).astype(kind)


def heavy_noise(rng, extent, width, bound, split, heavy, held_as=jnp.bfloat16):
    array = width * jax.random.normal(rng, extent, jnp.float32)
    if split:
        array = array * steps_of(rng, extent, split, -0.22, 0.18)
    return jnp.clip(spiked(array, jax.random.fold_in(rng, 3), *heavy), -bound, bound).astype(held_as)


def setup_inputs(seed: int = 0) -> dict:
    splits = jax.random.split(jax.random.key(seed), 22)
    return {
        "tokens": scatter_about(splits[0], (TOKENS, D), 1.0, 6.0, ((0, 8), (1, 16))),
        "lengths": uneven(splits[1], REQS, TOKENS, TOKENS // 4, 2).astype(jnp.int32),
        "deal": jax.random.permutation(splits[2], REQS).astype(jnp.int32),
        "pre_gain": jnp.clip(1.0 + 0.1 * jax.random.normal(splits[3], (D,), jnp.float32), 0.5, 1.5),
        "w_inner": draw_w_inner(jax.random.fold_in(splits[21], 71), 0),
        "w_group": scatter_about(splits[5], (D, 2, GROUPS, STATE), D ** -0.5, 0.09375, ((2, 4),)),
        "w_step": scatter_about(splits[6], (D, HEADS), D ** -0.5, 0.09375, ((1, 16),)),
        "conv_inner": jnp.clip(jax.random.uniform(splits[7], (KERNEL, E), jnp.float32, -0.5, 0.5) * steps_of(splits[7], (KERNEL, E), ((1, 16),), -0.4, 0.0), -0.5, 0.5),
        "conv_group": jnp.clip(jax.random.uniform(splits[8], (KERNEL, 2, GROUPS, STATE), jnp.float32, -0.5, 0.5) * steps_of(splits[8], (KERNEL, 2, GROUPS, STATE), ((2, 4),), -0.4, 0.0), -0.5, 0.5),
        "conv_bias_inner": jnp.clip(jax.random.uniform(splits[9], (E,), jnp.float32, -0.5, 0.5) * steps_of(splits[9], (E,), ((0, 16),), -0.4, 0.0), -0.5, 0.5),
        "conv_bias_group": jnp.clip(jax.random.uniform(splits[10], (2, GROUPS, STATE), jnp.float32, -0.5, 0.5) * steps_of(splits[10], (2, GROUPS, STATE), ((1, 4),), -0.4, 0.0), -0.5, 0.5),
        "edge_inner": scatter_about(splits[11], (REQS, KERNEL - 1, E), 1.0, 6.0, ((2, 16),)),
        "edge_group": scatter_about(splits[12], (REQS, KERNEL - 1, 2, GROUPS, STATE), 1.0, 6.0, ((3, 4),)),
        "init_states": scatter_about(splits[13], (REQS, HEADS, HEAD, STATE), (STATE ** -0.5), 1.25, ((1, 16),), jnp.float32),
        "step_bias": jnp.clip(-5.3 + 3.0000002 * jax.random.uniform(splits[14], (HEADS,), jnp.float32) ** steps_of(splits[14], (HEADS,), ((0, 16),), -0.2, 0.2), -5.3, -2.3),
        "decay_log": jnp.clip(-3.9 + 3.9 * jax.random.uniform(splits[15], (HEADS,), jnp.float32) ** steps_of(splits[15], (HEADS,), ((0, 16),), -0.2, 0.2), -3.9, 0.0),
        "skip": jnp.clip(0.5 + 1.0 * jax.random.uniform(splits[16], (HEADS,), jnp.float32) ** steps_of(splits[16], (HEADS,), ((0, 16),), -0.2, 0.2), 0.5, 1.5),
        "inner_gain": jnp.clip(1.0 + 0.1 * jax.random.normal(splits[17], (E,), jnp.float32), 0.5, 1.5),
        "w_out": heavy_noise(splits[18], (E, D), E ** -0.5, 0.09375, ((0, 16),), (0, 1, 16, 2.0)),
        "final_gain": jnp.clip(1.0 + 0.1 * jax.random.normal(splits[19], (D,), jnp.float32), 0.5, 1.5),
        "w_head": scatter_about(splits[20], (D, VOCAB), D ** -0.5, 0.09375, ((1, 128),)),
    }


EPSILON = 1e-05
HIGHEST = lax.Precision.HIGHEST

def rms_scale(values, axis):
    return lax.rsqrt(lax.optimization_barrier(jnp.mean(values * values, axis=axis)) + EPSILON)

def block_basics(log_block, seg_block, prev_block):
    running = jnp.cumsum(log_block, axis=0)
    flag = seg_block == prev_block[0]
    lower = jnp.arange(BLOCK)[:, None] >= jnp.arange(BLOCK)[None, :]
    same = (seg_block[:, None] == seg_block[None, :]) & lower
    first = seg_block != prev_block
    base = jnp.einsum('ts,sh->th', (same & first[None, :]).astype(jnp.float32), running - log_block, precision=HIGHEST)
    init_coef = jnp.where(flag[:, None], 0.0, jnp.exp(running - base))
    carry_coef = jnp.where(flag[:, None], jnp.exp(running), 0.0)
    return (running, same, init_coef, carry_coef)

def state_at(place, entry, x_block, key_heads, step_block, running, same, init_coef, carry_coef, seg_block, init_dealt):
    keep = same[place][:, None]
    decay_row = jnp.where(keep, jnp.exp(jnp.where(keep, running[place][None, :] - running, 0.0)), 0.0)
    share = (decay_row * step_block).astype(jnp.bfloat16)
    share = lax.optimization_barrier(share).astype(jnp.float32)
    term = jnp.einsum('sh,shp,shn->hpn', share, x_block.astype(jnp.float32), key_heads, precision=HIGHEST)
    chosen = init_dealt[seg_block[place]]
    return term + init_coef[place][:, None, None] * chosen + carry_coef[place][:, None, None] * entry

def reference(tokens, lengths, deal, pre_gain, w_inner, w_group, w_step, conv_inner, conv_group, conv_bias_inner, conv_bias_group, edge_inner, edge_group, init_states, step_bias, decay_log, skip, inner_gain, w_out, final_gain, w_head):
    wide = tokens.astype(jnp.float32)
    inv_rms = rms_scale(wide, 1)[:, None]
    scaled = (wide * pre_gain).astype(jnp.bfloat16)
    gate_x = jnp.dot(scaled, w_inner.reshape(D, 2 * E), preferred_element_type=jnp.float32) * inv_rms
    gate_in = gate_x[:, :E].astype(jnp.bfloat16)
    inner_in = gate_x[:, E:].astype(jnp.bfloat16)
    pair_width = 2 * GROUPS * STATE
    group_in = (jnp.dot(scaled, w_group.reshape(D, pair_width), preferred_element_type=jnp.float32) * inv_rms).astype(jnp.bfloat16)
    step_raw = jnp.dot(scaled, w_step, preferred_element_type=jnp.float32) * inv_rms
    ends = jnp.cumsum(lengths).astype(jnp.int32)
    begins = (ends - lengths).astype(jnp.int32)
    position = jnp.arange(TOKENS, dtype=jnp.int32)
    segment = (lax.optimization_barrier(jnp.sum((begins[None, :] <= position[:, None]).astype(jnp.int32), axis=1)) - 1).astype(jnp.int32)
    seg_before = (lax.optimization_barrier(jnp.sum((begins[None, :] < position[:, None]).astype(jnp.int32), axis=1)) - 1).astype(jnp.int32)
    offset = (position - begins[segment]).astype(jnp.int32)
    owner = deal[segment].astype(jnp.int32)
    channels = jnp.concatenate([inner_in, group_in], axis=1)
    conv_taps = jnp.concatenate([conv_inner, conv_group.reshape(KERNEL, pair_width)], axis=1)
    conv_shift = jnp.concatenate([conv_bias_inner, conv_bias_group.reshape(pair_width)])
    edges = jnp.concatenate([edge_inner, edge_group.reshape(REQS, KERNEL - 1, pair_width)], axis=2)
    summed = conv_shift + conv_taps[KERNEL - 1] * channels.astype(jnp.float32)
    for back in range(1, KERNEL):
        earlier = jnp.concatenate([jnp.zeros((back, channels.shape[1]), jnp.bfloat16), channels[:-back]], axis=0)
        slot = jnp.clip(KERNEL - 1 - back + offset, 0, KERNEL - 2).astype(jnp.int32)
        from_edge = edges[owner, slot]
        value = jnp.where((offset >= back)[:, None], earlier, from_edge)
        summed = summed + conv_taps[KERNEL - 1 - back] * value.astype(jnp.float32)
    mixed_in = jax.nn.silu(summed).astype(jnp.bfloat16)
    inner_x = mixed_in[:, :E].reshape(TOKENS, HEADS, HEAD)
    keys = mixed_in[:, E:E + GROUPS * STATE].reshape(TOKENS, GROUPS, STATE)
    queries = mixed_in[:, E + GROUPS * STATE:].reshape(TOKENS, GROUPS, STATE)
    step = jax.nn.softplus(step_raw + step_bias)
    log_decay = -jnp.exp(decay_log) * step
    init_dealt = init_states[deal]
    blocks = TOKENS // BLOCK
    repeat = HEADS // GROUPS

    def heads_of(grouped):
        return jnp.repeat(grouped.astype(jnp.float32), repeat, axis=1)

    def shaped(values):
        return values.reshape((blocks, BLOCK) + values.shape[1:])
    pieces = (shaped(inner_x), shaped(keys), shaped(queries), shaped(step), shaped(log_decay), shaped(segment), shaped(seg_before))

    def block_step(entry, block_pieces):
        x_block, key_block, query_block, step_block, log_block, seg_block, prev_block = block_pieces
        running, same, init_coef, carry_coef = block_basics(log_block, seg_block, prev_block)
        keep = same[:, :, None]
        diff = running[:, None, :] - running[None, :, :]
        decay = jnp.where(keep, jnp.exp(jnp.where(keep, diff, 0.0)), 0.0)
        scores = jnp.einsum('tgn,sgn->tsg', query_block.astype(jnp.float32), key_block.astype(jnp.float32), precision=HIGHEST)
        scores = jnp.repeat(scores, repeat, axis=2)
        weight = (scores * decay * step_block[None, :, :]).astype(jnp.bfloat16)
        weight = lax.optimization_barrier(weight).astype(jnp.float32)
        within = jnp.einsum('tsh,shp->thp', weight, x_block.astype(jnp.float32), precision=HIGHEST)
        query_heads = heads_of(query_block)

        def init_piece(piece_in):
            query_part, seg_part = piece_in
            return jnp.einsum('thn,thpn->thp', query_part, init_dealt[seg_part], precision=HIGHEST)
        init_dot = lax.map(init_piece, (query_heads.reshape(BLOCK // 16, 16, HEADS, STATE), seg_block.reshape(BLOCK // 16, 16)))
        init_dot = init_dot.reshape(BLOCK, HEADS, HEAD)
        carry_dot = jnp.einsum('thn,hpn->thp', query_heads, entry, precision=HIGHEST)
        result = within + init_coef[:, :, None] * init_dot
        result = result + carry_coef[:, :, None] * carry_dot
        result = result + skip[None, :, None] * x_block.astype(jnp.float32)
        leaving = state_at(BLOCK - 1, entry, x_block, heads_of(key_block), step_block, running, same, init_coef, carry_coef, seg_block, init_dealt)
        return (leaving, (result, entry))
    entry_zero = jnp.zeros((HEADS, HEAD, STATE), jnp.float32)
    _, (results, entries) = lax.scan(block_step, entry_zero, pieces)

    def final_of(request):
        last = ends[request] - 1
        which = (last // BLOCK).astype(jnp.int32)
        place = (last % BLOCK).astype(jnp.int32)

        def take(values):
            return lax.dynamic_index_in_dim(values, which, 0, keepdims=False)
        running, same, init_coef, carry_coef = block_basics(take(pieces[4]), take(pieces[5]), take(pieces[6]))
        return state_at(place, take(entries), take(pieces[0]), heads_of(take(pieces[1])), take(pieces[3]), running, same, init_coef, carry_coef, take(pieces[5]), init_dealt)
    finals = lax.map(final_of, jnp.arange(REQS, dtype=jnp.int32))
    final_states = jnp.zeros_like(init_states).at[deal].set(finals)
    y_flat = results.reshape(TOKENS, E)
    gated = y_flat * jax.nn.silu(gate_in.astype(jnp.float32))
    grouped = gated.reshape(TOKENS, GROUPS, E // GROUPS)
    normed = ((grouped * rms_scale(grouped, 2)[:, :, None]).reshape(TOKENS, E) * inner_gain).astype(jnp.bfloat16)
    mixed = jnp.dot(normed, w_out, preferred_element_type=jnp.float32)
    hidden_out = (wide + mixed).astype(jnp.bfloat16)
    last_rows = hidden_out[ends - 1].astype(jnp.float32)
    head_in = (last_rows * rms_scale(last_rows, 1)[:, None] * final_gain).astype(jnp.bfloat16)
    scores_out = jnp.dot(head_in, w_head, preferred_element_type=jnp.float32)
    logits = jnp.zeros((REQS, VOCAB), jnp.float32).at[deal].set(scores_out)
    return (hidden_out, final_states, logits)
```

```python
import jax
import jax.numpy as jnp
from jax import lax
from jax.experimental import pallas as pl
from jax.experimental.pallas import tpu as pltpu
from jax.sharding import PartitionSpec as P

BLOCK = 256


EPSILON = 1e-05
HIGHEST = lax.Precision.HIGHEST


def from_behind(block, axis, distance):
    devices = range(lax.axis_size(axis))
    route = [(i - distance, i) for i in devices if i - distance in devices]
    return lax.ppermute(block, axis, route)


def from_partner(x, axis, bit):
    return lax.ppermute(x, axis, [(i, i ^ 1 << bit) for i in range(lax.axis_size(axis))])


def pick_group(table, axis, which):
    return lax.dynamic_index_in_dim(table, which, axis, keepdims=False)


def exact_pairs(spread, keys_bf, form):
    upper = spread.astype(jnp.bfloat16)
    lower_part = (spread - upper.astype(jnp.float32)).astype(jnp.bfloat16)
    first_term = jnp.einsum(form, upper, keys_bf, preferred_element_type=jnp.float32)
    return first_term + jnp.einsum(form, lower_part, keys_bf, preferred_element_type=jnp.float32)


MESH = pl.DeviceIdType.MESH
HALF = 256
FEAT = 256
VMEM_LIMIT = 62 * 1024 * 1024


def spot(axis, shift):
    size = lax.axis_size(axis)
    return lax.rem(lax.axis_index(axis) + shift + size, size)


def block_of(half, du, dv):
    row = spot("row", dv + half * (du - dv))
    col = spot("col", du + half * (dv - du))
    return row * lax.axis_size("col") + col


def remote(src, dst, sends, recvs, place, axis, shift):
    return pltpu.make_async_remote_copy(
        src_ref=src,
        dst_ref=dst,
        send_sem=sends.at[place],
        recv_sem=recvs.at[place],
        device_id={axis: spot(axis, shift)},
        device_id_type=MESH,
    )


def greet(peers):
    barrier = pltpu.get_barrier_semaphore()
    for peer in peers:
        pl.semaphore_signal(barrier, inc=1, device_id=peer, device_id_type=MESH)
    pl.semaphore_wait(barrier, len(peers))


PLANE = (("row", 1), ("row", -1), ("col", 1), ("col", -1))
AXES = (("col", "row"), ("row", "col"))
ORDER = (0, -1, 1, 2)
CHUNK = 64
PARTS = 4


def project_kernel(
    tokens,
    w_inner,
    w_group,
    w_step,
    gain,
    gate_out,
    chan_out,
    step_out,
    raw_inner,
    raw_group,
    weights,
    wide_inner,
    wide_group,
    held,
    total,
    total_step,
    squares,
    load_sem,
    own_sem,
    sends,
    recvs,
):
    depth = weights.shape[0]
    width = gate_out.shape[1]
    lanes = 128
    rows_part = depth // PARTS
    flat_inner = w_inner.reshape(2 * depth, width)
    flat_group = w_group.reshape(4 * depth, lanes)
    loads = []
    for part in range(PARTS):
        loads.append(
            (
                pltpu.make_async_copy(
                    flat_inner.at[pl.ds(2 * rows_part * part, 2 * rows_part)],
                    raw_inner.at[pl.ds(2 * rows_part * part, 2 * rows_part)],
                    load_sem.at[0, part],
                ),
                pltpu.make_async_copy(
                    flat_group.at[pl.ds(4 * rows_part * part, 4 * rows_part)],
                    raw_group.at[pl.ds(4 * rows_part * part, 4 * rows_part)],
                    load_sem.at[1, part],
                ),
            )
        )
    own = block_of(0, 0, 0)
    own_copy = pltpu.make_async_copy(tokens, held.at[own], own_sem)
    own_copy.start()
    greet([{axis: spot(axis, shift)} for axis, shift in PLANE])
    messages = {}

    def send(half, number, du, dv, axis, shift, first, count, from_own=False):
        block = block_of(half, du, dv)
        rows = pl.ds(half * HALF + first, count)
        src = tokens.at[rows] if from_own else held.at[block, rows]
        copy = remote(
            src, held.at[block, rows], sends.at[half], recvs.at[half], number, axis, shift
        )
        copy.start()
        messages[half, number] = copy

    def arrive(half, *numbers):
        for number in numbers:
            messages[half, number].wait_recv()

    def spread(half, k, from_own=False):
        axis = AXES[half][1]
        send(half, 4 + 4 * k, ORDER[k], 0, axis, 1, 0, HALF, from_own)
        send(half, 5 + 4 * k, ORDER[k], 0, axis, -1, 0, HALF, from_own)

    def relay(half, k):
        axis = AXES[half][1]
        arrive(half, 4 + 4 * k)
        send(half, 6 + 4 * k, ORDER[k], -1, axis, 1, 0, HALF // 2)
        arrive(half, 5 + 4 * k)
        send(half, 7 + 4 * k, ORDER[k], 1, axis, -1, HALF // 2, HALF // 2)

    for half in (0, 1):
        axis = AXES[half][0]
        send(half, 0, 0, 0, axis, 1, 0, HALF, True)
        send(half, 1, 0, 0, axis, -1, 0, HALF, True)
    for half in (0, 1):
        spread(half, 0, True)
    for part in range(PARTS):
        loads[part][0].start()
        loads[part][1].start()
    group_local = lax.axis_index("col") * 2 // lax.axis_size("col")

    def untangle(part):
        loads[part][0].wait()
        loads[part][1].wait()

        def body(i, carry):
            base = pl.multiple_of(part * rows_part + i * CHUNK, CHUNK)
            for j in range(width // lanes):
                wide_inner[j] = raw_inner[
                    pl.ds(2 * base, 2 * CHUNK), j * lanes : (j + 1) * lanes
                ].astype(jnp.float32)
            wide_group[...] = raw_group[pl.ds(4 * base, 4 * CHUNK), :].astype(jnp.float32)
            for which in range(2):
                for j in range(width // lanes):
                    weights[
                        pl.ds(base, CHUNK), which * width + j * lanes : which * width + (j + 1) * lanes
                    ] = wide_inner[j, pl.ds(which, CHUNK, stride=2), :].astype(jnp.bfloat16)
                start = 2 * width + which * lanes
                weights[pl.ds(base, CHUNK), start : start + lanes] = wide_group[
                    pl.ds(2 * which + group_local, CHUNK, stride=4), :
                ].astype(jnp.bfloat16)
            return carry

        lax.fori_loop(0, rows_part // CHUNK, body, 0)

    total[...] = jnp.zeros_like(total)
    total_step[...] = jnp.zeros_like(total_step)
    squares[...] = jnp.zeros_like(squares)

    def multiply(half, du, dv):
        block = block_of(half, du, dv)
        rows = pl.ds(pl.multiple_of(half * HALF, HALF), HALF)
        column = pl.multiple_of(block * FEAT, FEAT)
        wide = held[block, rows, :].astype(jnp.float32)
        squares[rows, :] += wide[:, :lanes] * wide[:, :lanes] + wide[:, lanes:] * wide[:, lanes:]
        scaled = (wide * gain[:, pl.ds(column, FEAT)]).astype(jnp.bfloat16)
        total[rows, :] += jnp.dot(
            scaled, weights[pl.ds(column, FEAT), :], preferred_element_type=jnp.float32
        )
        total_step[rows, :] += lax.dot_general(
            scaled,
            w_step[:, pl.ds(column, FEAT)],
            (((1,), (1,)), ((), ())),
            preferred_element_type=jnp.float32,
        )

    def run(count, pick):
        def body(i, carry):
            half = lax.rem(i, 2)
            du, dv = pick(i // 2)
            multiply(half, du, dv)
            return carry

        lax.fori_loop(0, 2 * count, body, 0)

    untangle(0)
    for half in (0, 1):
        arrive(half, 0)
        send(half, 2, -1, 0, AXES[half][0], 1, 0, HALF // 2)
        spread(half, 1)
        arrive(half, 1)
        send(half, 3, 1, 0, AXES[half][0], -1, HALF // 2, HALF // 2)
        spread(half, 2)
    untangle(1)
    for half in (0, 1):
        relay(half, 0)
    untangle(2)
    for half in (0, 1):
        arrive(half, 2, 3)
        spread(half, 3)
    untangle(3)
    own_copy.wait()
    run(2, lambda j: (j, 0))
    for half in (0, 1):
        relay(half, 1)
    run(2, lambda j: (j + 2, 0))
    for half in (0, 1):
        relay(half, 2)
    run(4, lambda j: (-(j // 2), 2 * lax.rem(j, 2) - 1))
    for half in (0, 1):
        relay(half, 3)
    run(4, lambda j: (1 + j // 2, 2 * lax.rem(j, 2) - 1))
    for half in (0, 1):
        for k in range(4):
            arrive(half, 6 + 4 * k, 7 + 4 * k)
    run(4, lambda j: (j, 2))
    for half in (0, 1):
        for number in range(20):
            messages[half, number].wait_send()
    inv_rms = lax.rsqrt(jnp.sum(squares[...], axis=1, keepdims=True) / depth + EPSILON)
    gate_out[...] = (total[:, :width] * inv_rms).astype(jnp.bfloat16)
    chan_out[...] = (total[:, width:] * inv_rms).astype(jnp.bfloat16)
    step_out[...] = total_step[...] * inv_rms


def project(tokens, w_inner, w_group, w_step, pre_gain):
    rows, feat = tokens.shape
    depth, _, width = w_inner.shape
    heads = w_step.shape[1]
    state = w_group.shape[3]
    blocks = depth // feat
    columns = 2 * width + 2 * state
    vmem = pl.BlockSpec(memory_space=pltpu.VMEM)
    anywhere = pl.BlockSpec(memory_space=pl.ANY)
    return pl.pallas_call(
        project_kernel,
        out_shape=[
            jax.ShapeDtypeStruct((rows, width), jnp.bfloat16),
            jax.ShapeDtypeStruct((rows, width + 2 * state), jnp.bfloat16),
            jax.ShapeDtypeStruct((rows, heads), jnp.float32),
        ],
        in_specs=[anywhere, anywhere, anywhere, vmem, vmem],
        out_specs=[vmem] * 3,
        scratch_shapes=[
            pltpu.VMEM((2 * depth, width), jnp.bfloat16),
            pltpu.VMEM((4 * depth, state), jnp.bfloat16),
            pltpu.VMEM((depth, columns), jnp.bfloat16),
            pltpu.VMEM((width // 128, 2 * CHUNK, 128), jnp.float32),
            pltpu.VMEM((4 * CHUNK, 128), jnp.float32),
            pltpu.VMEM((blocks, rows, feat), jnp.bfloat16),
            pltpu.VMEM((rows, columns), jnp.float32),
            pltpu.VMEM((rows, heads), jnp.float32),
            pltpu.VMEM((rows, 128), jnp.float32),
            pltpu.SemaphoreType.DMA((2, PARTS)),
            pltpu.SemaphoreType.DMA,
            pltpu.SemaphoreType.DMA((2, 20)),
            pltpu.SemaphoreType.DMA((2, 20)),
        ],
        compiler_params=pltpu.CompilerParams(
            collective_id=0, has_side_effects=True, vmem_limit_bytes=VMEM_LIMIT
        ),
        name="project",
    )(tokens, w_inner, w_group, w_step.T, pre_gain[None, :])


SPREAD = (2, 1, -1, 0)


def slot_ends(lengths, deal, first_row, shape, dim):
    requests = lengths.shape[0]
    slots = lax.broadcasted_iota(jnp.int32, shape, dim)
    ends = jnp.zeros(shape, jnp.int32)
    end = -1 - first_row
    for k in range(requests):
        end = end + lengths[k]
        ends = jnp.where(slots == deal[k], end, ends)
    return ends


def finish_kernel(
    lengths,
    deal,
    normed,
    w_out,
    tokens,
    w_head,
    final_gain,
    hidden,
    logits,
    weights,
    head,
    partials,
    stage_far,
    stage_near,
    land_far,
    land_near,
    stage_far2,
    stage_near2,
    land_far2,
    land_near2,
    picks,
    rows_all,
    wide_rows,
    load_sem,
    sends,
    recvs,
    pick_sends,
    pick_recvs,
    row_sends,
    row_recvs,
):
    rows, feat = tokens.shape
    requests = lengths.shape[0]
    seq = lax.axis_size("seq")
    load_out = pltpu.make_async_copy(w_out, weights, load_sem.at[0])
    load_head = pltpu.make_async_copy(w_head, head, load_sem.at[1])
    load_out.start()
    load_head.start()
    plane = [(dr, dc) for dr in range(4) for dc in range(4) if dr or dc]
    peers = [{axis: spot(axis, shift)} for axis, shift in PLANE]
    peers += [{"seq": spot("seq", shift)} for shift in range(1, seq)]
    peers += [
        {"row": spot("row", dr), "col": spot("col", dc)}
        for dr, dc in plane
        if not ((dr == 0 and dc != 2) or (dc == 0 and dr != 2))
    ]
    greet(peers)
    load_out.wait()

    def compute(first, count):
        def body(i, carry):
            half = lax.rem(i, 2)
            j = i // 2 + first
            dv = 2 - j // 4 - j // 8 + (j // 12) * 2
            du = 2 - lax.rem(j, 4) - lax.rem(j, 4) // 2 + (lax.rem(j, 4) // 3) * 2
            block = block_of(half, du, dv)
            partials[half, j] = jnp.dot(
                normed[pl.ds(pl.multiple_of(half * HALF, HALF), HALF), :],
                weights[:, pl.ds(pl.multiple_of(block * feat, feat), feat)],
                preferred_element_type=jnp.float32,
            )
            return carry

        lax.fori_loop(0, 2 * count, body, 0)

    started = {}

    def send(half, number, src, dst, axis, shift):
        copy = remote(src, dst, sends.at[half], recvs.at[half], number, axis, shift)
        copy.start()
        started[half, number] = copy

    def far(half, values, stage, land, number, axis):
        for side in (0, 1):
            stage[side] = values[side * 128 : side * 128 + 128].astype(jnp.bfloat16)
            send(half, number + side, stage.at[side], land.at[side], axis, 1 - 2 * side)

    def near(half, side, values, far_land, far_number, stage, land, number, axis):
        started[half, far_number + side].wait_recv()
        extra = far_land[side].astype(jnp.float32)
        keep = slice(128 - 128 * side, 256 - 128 * side)
        mix = slice(128 * side, 128 * side + 128)
        stage[side, mix] = (values[mix] + extra).astype(jnp.bfloat16)
        stage[side, keep] = values[keep].astype(jnp.bfloat16)
        send(half, number + side, stage.at[side], land.at[side], axis, 1 - 2 * side)

    compute(0, 4)
    for k in range(4):
        for half in (0, 1):
            far(
                half,
                partials[half, k],
                stage_far.at[half, k],
                land_far.at[half, k],
                2 * k,
                AXES[half][1],
            )
    compute(4, 12)
    for k in range(4):
        for half in (0, 1):
            for side in (0, 1):
                near(
                    half,
                    side,
                    partials[half, 4 + 4 * side + k],
                    land_far.at[half, k],
                    2 * k,
                    stage_near.at[half, k],
                    land_near.at[half, k],
                    8 + 2 * k,
                    AXES[half][1],
                )
    for k in range(4):
        for half in (0, 1):
            axis = AXES[half][0]
            total = partials[half, 12 + k]
            for side in (0, 1):
                started[half, 8 + 2 * k + side].wait_recv()
                total = total + land_near[half, k, side].astype(jnp.float32)
            if k == 0:
                far(half, total, stage_far2.at[half], land_far2.at[half], 16, axis)
            elif k < 3:
                near(
                    half,
                    k - 1,
                    total,
                    land_far2.at[half],
                    16,
                    stage_near2.at[half],
                    land_near2.at[half],
                    18,
                    axis,
                )
            else:
                for side in (0, 1):
                    started[half, 18 + side].wait_recv()
                    total = total + land_near2[half, side].astype(jnp.float32)
                place = slice(half * HALF, half * HALF + HALF)
                hidden[place, :] = (tokens[place, :].astype(jnp.float32) + total).astype(
                    jnp.bfloat16
                )
    first_row = lax.axis_index("seq") * rows
    ends = slot_ends(lengths, deal, first_row, (requests, rows), 0)
    chooser = (ends == lax.broadcasted_iota(jnp.int32, (requests, rows), 1)).astype(jnp.bfloat16)
    picks[0] = jnp.dot(chooser, hidden[...], preferred_element_type=jnp.float32).astype(
        jnp.bfloat16
    )
    handed = []
    for shift in range(1, seq):
        copy = remote(
            picks.at[0], picks.at[shift], pick_sends, pick_recvs, shift, "seq", shift
        )
        copy.start()
        handed.append(copy)
    for copy in handed:
        copy.wait_recv()
    whole = picks[0].astype(jnp.float32)
    for shift in range(1, seq):
        whole = whole + picks[shift].astype(jnp.float32)
    own = block_of(0, 0, 0)
    rows_all[own] = whole.astype(jnp.bfloat16)
    for number, (dr, dc) in enumerate(plane):
        copy = pltpu.make_async_remote_copy(
            src_ref=rows_all.at[own],
            dst_ref=rows_all.at[own],
            send_sem=row_sends.at[number],
            recv_sem=row_recvs.at[number],
            device_id={"row": spot("row", dr), "col": spot("col", dc)},
            device_id_type=MESH,
        )
        copy.start()
        handed.append(copy)
    for copy in handed[seq - 1 :]:
        copy.wait_recv()
    load_head.wait()
    total = jnp.zeros((requests, 128), jnp.float32)
    for block in range(len(plane) + 1):
        value = rows_all[block].astype(jnp.float32)
        wide_rows[:, block * feat : (block + 1) * feat] = value
        total = total + value[:, :128] * value[:, :128] + value[:, 128:] * value[:, 128:]
    depth = w_head.shape[0]
    scale = lax.rsqrt(jnp.sum(total, axis=1, keepdims=True) / depth + EPSILON)
    head_in = (wide_rows[...] * scale * final_gain[...]).astype(jnp.bfloat16)
    logits[...] = jnp.dot(head_in, head[...], preferred_element_type=jnp.float32)
    for copy in handed:
        copy.wait_send()
    for copy in started.values():
        copy.wait_send()


def finish(lengths, deal, normed, w_out, tokens, w_head, final_gain):
    rows, feat = tokens.shape
    inner, depth = w_out.shape
    requests = lengths.shape[0]
    vocab = w_head.shape[1]
    seq = lax.axis_size("seq")
    smem = pl.BlockSpec(memory_space=pltpu.SMEM)
    vmem = pl.BlockSpec(memory_space=pltpu.VMEM)
    anywhere = pl.BlockSpec(memory_space=pl.ANY)
    bf = jnp.bfloat16
    return pl.pallas_call(
        finish_kernel,
        out_shape=[
            jax.ShapeDtypeStruct((rows, feat), bf),
            jax.ShapeDtypeStruct((requests, vocab), jnp.float32),
        ],
        in_specs=[smem, smem, vmem, anywhere, vmem, anywhere, vmem],
        out_specs=[vmem, vmem],
        scratch_shapes=[
            pltpu.VMEM((inner, depth), bf),
            pltpu.VMEM((depth, vocab), bf),
            pltpu.VMEM((2, 16, HALF, feat), jnp.float32),
            pltpu.VMEM((2, 4, 2, 128, feat), bf),
            pltpu.VMEM((2, 4, 2, 256, feat), bf),
            pltpu.VMEM((2, 4, 2, 128, feat), bf),
            pltpu.VMEM((2, 4, 2, 256, feat), bf),
            pltpu.VMEM((2, 2, 128, feat), bf),
            pltpu.VMEM((2, 2, 256, feat), bf),
            pltpu.VMEM((2, 2, 128, feat), bf),
            pltpu.VMEM((2, 2, 256, feat), bf),
            pltpu.VMEM((seq, requests, feat), bf),
            pltpu.VMEM((16, requests, feat), bf),
            pltpu.VMEM((requests, depth), jnp.float32),
            pltpu.SemaphoreType.DMA((2,)),
            pltpu.SemaphoreType.DMA((2, 20)),
            pltpu.SemaphoreType.DMA((2, 20)),
            pltpu.SemaphoreType.DMA((seq,)),
            pltpu.SemaphoreType.DMA((seq,)),
            pltpu.SemaphoreType.DMA((15,)),
            pltpu.SemaphoreType.DMA((15,)),
        ],
        compiler_params=pltpu.CompilerParams(
            collective_id=1, has_side_effects=True, vmem_limit_bytes=VMEM_LIMIT
        ),
        name="finish",
    )(lengths, deal, normed, w_out, tokens, w_head, final_gain[None, :])


def per_device(
    tokens,
    lengths,
    deal,
    pre_gain,
    w_inner,
    w_group,
    w_step,
    conv_inner,
    conv_group,
    conv_bias_inner,
    conv_bias_group,
    edge_inner,
    edge_group,
    init_states,
    step_bias,
    decay_log,
    skip,
    inner_gain,
    w_out,
    final_gain,
    w_head,
):
    rows = tokens.shape[0]
    model_width = pre_gain.shape[0]
    requests = lengths.shape[0]
    kernel = conv_inner.shape[0]
    inner_dev = w_inner.shape[2]
    heads_dev = w_step.shape[1]
    head_size = inner_dev // heads_dev
    state_size = w_group.shape[3]
    group_local = lax.axis_index("col") * w_group.shape[2] // lax.axis_size("col")
    gate_in, channels, step_raw = project(tokens, w_inner, w_group, w_step, pre_gain)
    ends = jnp.cumsum(lengths)
    begins = ends - lengths
    first_row = lax.axis_index("seq") * rows
    position = first_row + jnp.arange(rows, dtype=jnp.int32)
    segment = jnp.sum((begins[None, :] <= position[:, None]).astype(jnp.int32), axis=1) - 1
    seg_before = jnp.sum((begins[None, :] < position[:, None]).astype(jnp.int32), axis=1) - 1
    member = segment[:, None] == jnp.arange(requests, dtype=jnp.int32)[None, :]
    offset = position - jnp.sum(jnp.where(member, begins[None, :], 0), axis=1)
    owner = jnp.sum(jnp.where(member, deal[None, :], 0), axis=1)
    width_all = channels.shape[1]
    conv_taps = jnp.concatenate(
        [conv_inner, jnp.reshape(pick_group(conv_group, 2, group_local), (kernel, 2 * state_size))],
        axis=1,
    )
    conv_shift = jnp.concatenate(
        [
            conv_bias_inner,
            jnp.reshape(pick_group(conv_bias_group, 1, group_local), (2 * state_size,)),
        ]
    )
    edges = jnp.concatenate(
        [
            edge_inner,
            jnp.reshape(
                pick_group(edge_group, 3, group_local), (requests, kernel - 1, 2 * state_size)
            ),
        ],
        axis=2,
    )
    edges = jnp.reshape(edges, (requests * (kernel - 1), width_all))
    rim = from_behind(channels[rows - (kernel - 1) :], "seq", 1)
    extended = jnp.concatenate([rim, channels], axis=0)
    summed = conv_shift + conv_taps[kernel - 1] * channels.astype(jnp.float32)
    slots = jnp.arange(requests * (kernel - 1), dtype=jnp.int32)
    for back in range(1, kernel):
        earlier = extended[kernel - 1 - back : kernel - 1 - back + rows]
        slot = owner * (kernel - 1) + (kernel - 1 - back) + offset
        lookup = ((slot[:, None] == slots[None, :]) & (offset < back)[:, None]).astype(jnp.bfloat16)
        from_edge = jnp.dot(lookup, edges, preferred_element_type=jnp.float32)
        value = jnp.where((offset >= back)[:, None], earlier.astype(jnp.float32), from_edge)
        summed = summed + conv_taps[kernel - 1 - back] * value
    mixed_in = jax.nn.silu(summed).astype(jnp.bfloat16)
    blocks = rows // BLOCK
    inner_x = jnp.reshape(mixed_in[:, :inner_dev], (blocks, BLOCK, heads_dev, head_size))
    keys = jnp.reshape(mixed_in[:, inner_dev : inner_dev + state_size], (blocks, BLOCK, state_size))
    queries = jnp.reshape(mixed_in[:, inner_dev + state_size :], (blocks, BLOCK, state_size))
    step = jax.nn.softplus(step_raw + step_bias)
    log_decay = -jnp.exp(decay_log) * step
    step_blocks = jnp.reshape(step, (blocks, BLOCK, heads_dev))
    log_blocks = jnp.reshape(log_decay, (blocks, BLOCK, heads_dev))
    running = jnp.cumsum(log_blocks, axis=1)
    seg_blocks = jnp.reshape(segment, (blocks, BLOCK))
    prev_blocks = jnp.reshape(seg_before, (blocks, BLOCK))
    flag = seg_blocks == prev_blocks[:, :1]
    lower = jnp.arange(BLOCK)[:, None] >= jnp.arange(BLOCK)[None, :]
    same = (seg_blocks[:, :, None] == seg_blocks[:, None, :]) & lower[None]
    first = seg_blocks != prev_blocks
    base = jnp.einsum(
        "cts,csh->cth",
        (same & first[:, None, :]).astype(jnp.float32),
        running - log_blocks,
        precision=HIGHEST,
    )
    keep = same[..., None]
    diff = running[:, :, None, :] - running[:, None, :, :]
    decay = jnp.where(keep, jnp.exp(jnp.where(keep, diff, 0.0)), 0.0)
    scores = jnp.einsum("ctn,csn->cts", queries, keys, preferred_element_type=jnp.float32)
    weight = (scores[..., None] * decay * step_blocks[:, None, :, :]).astype(jnp.bfloat16)
    within = jnp.einsum("ctsh,cshp->cthp", weight, inner_x, preferred_element_type=jnp.float32)
    dealing = (deal[:, None] == jnp.arange(requests, dtype=jnp.int32)[None, :]).astype(jnp.float32)
    init_dealt = jnp.reshape(
        jnp.dot(dealing, jnp.reshape(init_states, (requests, -1)), precision=HIGHEST),
        init_states.shape,
    )
    member_blocks = jnp.reshape(member.astype(jnp.float32), (blocks, BLOCK, requests))
    query_wide = queries.astype(jnp.float32)
    picked = jnp.where(
        jnp.reshape(member, (blocks, BLOCK, requests))[..., None],
        queries[:, :, None, :],
        jnp.zeros((), jnp.bfloat16),
    )
    init_high = init_dealt.astype(jnp.bfloat16)
    init_rest = init_dealt - init_high.astype(jnp.float32)
    init_mid = init_rest.astype(jnp.bfloat16)
    init_low = (init_rest - init_mid.astype(jnp.float32)).astype(jnp.bfloat16)
    init_dot = jnp.einsum("ctrn,rhpn->cthp", picked, init_high, preferred_element_type=jnp.float32)
    init_dot = init_dot + jnp.einsum(
        "ctrn,rhpn->cthp", picked, init_mid, preferred_element_type=jnp.float32
    )
    init_dot = init_dot + jnp.einsum(
        "ctrn,rhpn->cthp", picked, init_low, preferred_element_type=jnp.float32
    )
    init_coef = jnp.where(flag[..., None], 0.0, jnp.exp(running - base))
    carry_coef = jnp.where(flag[..., None], jnp.exp(running), 0.0)
    local_y = within + init_coef[..., None] * init_dot
    end_local = ends - 1 - first_row
    local_pos = jnp.reshape(jnp.arange(rows, dtype=jnp.int32), (blocks, BLOCK))
    select = (local_pos[:, None, :] == end_local[None, :, None]).astype(jnp.float32)
    block_pick = jnp.sum(select, axis=2)
    sel_init = jnp.einsum("cjt,cth->cjh", select, init_coef, precision=HIGHEST)
    sel_carry = jnp.einsum("cjt,cth->cjh", select, carry_coef, precision=HIGHEST)
    sel_member = jnp.einsum("cjt,ctr->cjr", select, member_blocks, precision=HIGHEST)
    sel_inits = jnp.einsum("cjr,rhpn->cjhpn", sel_member, init_dealt, precision=HIGHEST)
    decay_req = jnp.einsum("cjt,ctsh->jsh", select, decay, precision=HIGHEST)
    step_req = jnp.einsum("cj,csh->jsh", block_pick, step_blocks, precision=HIGHEST)
    pick_bf = block_pick.astype(jnp.bfloat16)
    x_req = jnp.einsum(
        "cj,cshp->jshp", pick_bf, inner_x, preferred_element_type=jnp.float32
    ).astype(jnp.bfloat16)
    keys_req = jnp.einsum("cj,csn->jsn", pick_bf, keys, preferred_element_type=jnp.float32).astype(
        jnp.bfloat16
    )
    share_req = (decay_req * step_req).astype(jnp.bfloat16)
    share_req = lax.optimization_barrier(share_req).astype(jnp.float32)
    spread_req = share_req[..., None] * x_req.astype(jnp.float32)
    local_req = exact_pairs(spread_req, keys_req, "jshp,jsn->jhpn")
    share_last = (decay[:, BLOCK - 1] * step_blocks).astype(jnp.bfloat16)
    share_last = lax.optimization_barrier(share_last).astype(jnp.float32)
    spread_last = share_last[..., None] * inner_x.astype(jnp.float32)
    last_state = exact_pairs(spread_last, keys, "cshp,csn->chpn")
    last_init = init_coef[:, BLOCK - 1]
    last_member = member_blocks[:, BLOCK - 1]
    last_inits = jnp.einsum("cr,rhpn->chpn", last_member, init_dealt, precision=HIGHEST)
    last_state = last_state + last_init[..., None, None] * last_inits
    last_carry = carry_coef[:, BLOCK - 1]
    gain_run = jnp.ones((heads_dev,), jnp.float32)
    state_run = jnp.zeros((heads_dev, head_size, state_size), jnp.float32)
    gain_list = []
    state_list = []
    for block in range(blocks):
        gain_list.append(gain_run)
        state_list.append(state_run)
        factor = last_carry[block]
        gain_run = factor * gain_run
        state_run = factor[:, None, None] * state_run + last_state[block]

    entry_dev = from_behind(state_run, "seq", 1)
    entry_dev = entry_dev + from_behind(gain_run, "seq", 1)[:, None, None] * from_behind(
        state_run, "seq", 2
    )
    entries = jnp.stack(gain_list)[:, :, None, None] * entry_dev[None] + jnp.stack(state_list)
    carry_dot = jnp.einsum("ctn,chpn->cthp", query_wide, entries, precision=HIGHEST)
    outputs = local_y + carry_coef[..., None] * carry_dot
    outputs = outputs + skip[:, None] * inner_x.astype(jnp.float32)
    finals = local_req + jnp.sum(sel_init[..., None, None] * sel_inits, axis=0)
    finals = finals + jnp.sum(sel_carry[..., None, None] * entries[:, None], axis=0)
    owned = jnp.reshape(
        jnp.dot(dealing.T, jnp.reshape(finals, (requests, -1)), precision=HIGHEST), finals.shape
    )
    final_states = lax.psum_scatter(owned, "seq", scatter_dimension=0, tiled=True)
    y_flat = jnp.reshape(outputs, (rows, inner_dev))
    gated = y_flat * jax.nn.silu(gate_in.astype(jnp.float32))
    own_squares = jnp.sum(gated * gated, axis=1)
    other_squares = from_partner(own_squares, "col", 0)
    norm_scale = lax.rsqrt((own_squares + other_squares) / (2 * inner_dev) + EPSILON)
    normed = (gated * norm_scale[:, None] * inner_gain).astype(jnp.bfloat16)
    hidden_out, logits = finish(lengths, deal, normed, w_out, tokens, w_head, final_gain)
    return (hidden_out, final_states, logits)


def solution(mesh):
    in_specs = (
        P("seq", ("row", "col")),
        P(),
        P(),
        P(),
        P(None, None, ("row", "col")),
        P(None, None, "row", None),
        P(None, ("row", "col")),
        P(None, ("row", "col")),
        P(None, None, "row", None),
        P(("row", "col")),
        P(None, "row", None),
        P(None, None, ("row", "col")),
        P(None, None, None, "row", None),
        P(None, ("row", "col"), None, None),
        P(("row", "col")),
        P(("row", "col")),
        P(("row", "col")),
        P(("row", "col")),
        P(("row", "col"), None),
        P(),
        P(None, ("seq", "row", "col")),
    )
    out_specs = (
        P("seq", ("row", "col")),
        P("seq", ("row", "col"), None, None),
        P(None, ("seq", "row", "col")),
    )
    return jax.shard_map(
        per_device, mesh=mesh, in_specs=in_specs, out_specs=out_specs, check_vma=False
    )
```

```python
import jax
import jax.numpy as jnp
from jax import lax
from jax.experimental import pallas as pl
from jax.experimental.pallas import tpu as pltpu
from jax.sharding import PartitionSpec as P

BLOCK = 256


EPSILON = 1e-05


MESH = pl.DeviceIdType.MESH
HALF = 256
FEAT = 256
VMEM_LIMIT = 62 * 1024 * 1024


def spot(axis, shift):
    size = lax.axis_size(axis)
    return lax.rem(lax.axis_index(axis) + shift + size, size)


def block_of(half, du, dv):
    row = spot("row", dv + half * (du - dv))
    col = spot("col", du + half * (dv - du))
    return row * lax.axis_size("col") + col


def remote(src, dst, sends, recvs, place, axis, shift):
    return pltpu.make_async_remote_copy(
        src_ref=src,
        dst_ref=dst,
        send_sem=sends.at[place],
        recv_sem=recvs.at[place],
        device_id={axis: spot(axis, shift)},
        device_id_type=MESH,
    )


def greet(peers):
    barrier = pltpu.get_barrier_semaphore()
    for peer in peers:
        pl.semaphore_signal(barrier, inc=1, device_id=peer, device_id_type=MESH)
    pl.semaphore_wait(barrier, len(peers))


PLANE = (("row", 1), ("row", -1), ("col", 1), ("col", -1))
AXES = (("col", "row"), ("row", "col"))
ORDER = (0, -1, 1, 2)
CHUNK = 64
PARTS = 4


def project_kernel(
    tokens,
    w_inner,
    w_group,
    w_step,
    gain,
    gate_out,
    chan_out,
    step_out,
    rim_out,
    raw_inner,
    raw_group,
    weights,
    wide_inner,
    wide_group,
    held,
    total,
    total_step,
    squares,
    load_sem,
    own_sem,
    sends,
    recvs,
    rim_stage,
    rim_land,
    rim_sems,
):
    depth = weights.shape[0]
    width = gate_out.shape[1]
    lanes = 128
    rows_part = depth // PARTS
    flat_inner = w_inner.reshape(2 * depth, width)
    flat_group = w_group.reshape(4 * depth, lanes)
    loads = []
    for part in range(PARTS):
        loads.append(
            (
                pltpu.make_async_copy(
                    flat_inner.at[pl.ds(2 * rows_part * part, 2 * rows_part)],
                    raw_inner.at[pl.ds(2 * rows_part * part, 2 * rows_part)],
                    load_sem.at[0, part],
                ),
                pltpu.make_async_copy(
                    flat_group.at[pl.ds(4 * rows_part * part, 4 * rows_part)],
                    raw_group.at[pl.ds(4 * rows_part * part, 4 * rows_part)],
                    load_sem.at[1, part],
                ),
            )
        )
    for part in range(PARTS):
        loads[part][0].start()
        loads[part][1].start()
    own = block_of(0, 0, 0)
    own_copy = pltpu.make_async_copy(tokens, held.at[own], own_sem)
    own_copy.start()
    greet([{axis: spot(axis, shift)} for axis, shift in PLANE + (("seq", 1), ("seq", -1))])
    messages = {}

    def send(half, number, du, dv, axis, shift, first, count, from_own=False):
        block = block_of(half, du, dv)
        rows = pl.ds(half * HALF + first, count)
        src = tokens.at[rows] if from_own else held.at[block, rows]
        copy = remote(
            src, held.at[block, rows], sends.at[half], recvs.at[half], number, axis, shift
        )
        copy.start()
        messages[half, number] = copy

    def arrive(half, *numbers):
        for number in numbers:
            messages[half, number].wait_recv()

    def spread(half, k, from_own=False):
        axis = AXES[half][1]
        send(half, 4 + 4 * k, ORDER[k], 0, axis, 1, 0, HALF, from_own)
        send(half, 5 + 4 * k, ORDER[k], 0, axis, -1, 0, HALF, from_own)

    def relay(half, k):
        axis = AXES[half][1]
        arrive(half, 4 + 4 * k)
        send(half, 6 + 4 * k, ORDER[k], -1, axis, 1, 0, HALF // 2)
        arrive(half, 5 + 4 * k)
        send(half, 7 + 4 * k, ORDER[k], 1, axis, -1, HALF // 2, HALF // 2)

    for half in (0, 1):
        axis = AXES[half][0]
        send(half, 0, 0, 0, axis, 1, 0, HALF, True)
        send(half, 1, 0, 0, axis, -1, 0, HALF, True)
    for half in (0, 1):
        spread(half, 0, True)
    group_local = lax.axis_index("col") * 2 // lax.axis_size("col")

    def untangle(part):
        loads[part][0].wait()
        loads[part][1].wait()

        def body(i, carry):
            base = pl.multiple_of(part * rows_part + i * CHUNK, CHUNK)
            for j in range(width // lanes):
                wide_inner[j] = raw_inner[
                    pl.ds(2 * base, 2 * CHUNK), j * lanes : (j + 1) * lanes
                ].astype(jnp.float32)
            wide_group[...] = raw_group[pl.ds(4 * base, 4 * CHUNK), :].astype(jnp.float32)
            for which in range(2):
                for j in range(width // lanes):
                    weights[
                        pl.ds(base, CHUNK), which * width + j * lanes : which * width + (j + 1) * lanes
                    ] = wide_inner[j, pl.ds(which, CHUNK, stride=2), :].astype(jnp.bfloat16)
                start = 2 * width + which * lanes
                weights[pl.ds(base, CHUNK), start : start + lanes] = wide_group[
                    pl.ds(2 * which + group_local, CHUNK, stride=4), :
                ].astype(jnp.bfloat16)
            return carry

        lax.fori_loop(0, rows_part // CHUNK, body, 0)

    total[...] = jnp.zeros_like(total)
    total_step[...] = jnp.zeros_like(total_step)
    squares[...] = jnp.zeros_like(squares)

    def multiply(half, du, dv):
        block = block_of(half, du, dv)
        rows = pl.ds(pl.multiple_of(half * HALF, HALF), HALF)
        column = pl.multiple_of(block * FEAT, FEAT)
        wide = held[block, rows, :].astype(jnp.float32)
        squares[rows, :] += wide[:, :lanes] * wide[:, :lanes] + wide[:, lanes:] * wide[:, lanes:]
        scaled = (wide * gain[:, pl.ds(column, FEAT)]).astype(jnp.bfloat16)
        total[rows, :] += jnp.dot(
            scaled, weights[pl.ds(column, FEAT), :], preferred_element_type=jnp.float32
        )
        total_step[rows, :] += lax.dot_general(
            scaled,
            w_step[:, pl.ds(column, FEAT)],
            (((1,), (1,)), ((), ())),
            preferred_element_type=jnp.float32,
        )

    def run(count, pick):
        def body(i, carry):
            half = lax.rem(i, 2)
            du, dv = pick(i // 2)
            multiply(half, du, dv)
            return carry

        lax.fori_loop(0, 2 * count, body, 0)

    untangle(0)
    for half in (0, 1):
        arrive(half, 0)
        send(half, 2, -1, 0, AXES[half][0], 1, 0, HALF // 2)
        spread(half, 1)
        arrive(half, 1)
        send(half, 3, 1, 0, AXES[half][0], -1, HALF // 2, HALF // 2)
        spread(half, 2)
    untangle(1)
    for half in (0, 1):
        relay(half, 0)
    untangle(2)
    for half in (0, 1):
        arrive(half, 2, 3)
        spread(half, 3)
    untangle(3)
    own_copy.wait()
    run(2, lambda j: (j, 0))
    for half in (0, 1):
        relay(half, 1)
    run(2, lambda j: (j + 2, 0))
    for half in (0, 1):
        relay(half, 2)
    run(4, lambda j: (-(j // 2), 2 * lax.rem(j, 2) - 1))
    for half in (0, 1):
        relay(half, 3)
    run(4, lambda j: (1 + j // 2, 2 * lax.rem(j, 2) - 1))
    for half in (0, 1):
        for k in range(4):
            arrive(half, 6 + 4 * k, 7 + 4 * k)
    run(4, lambda j: (j, 2))
    for half in (0, 1):
        for number in range(20):
            messages[half, number].wait_send()
    inv_rms = lax.rsqrt(jnp.sum(squares[...], axis=1, keepdims=True) / depth + EPSILON)
    last = total.shape[0] - rim_stage.shape[0]
    rim_stage[...] = (total[last:, width:] * inv_rms[last:]).astype(jnp.bfloat16)
    rim_copy = pltpu.make_async_remote_copy(
        src_ref=rim_stage,
        dst_ref=rim_land,
        send_sem=rim_sems.at[0],
        recv_sem=rim_sems.at[1],
        device_id={"seq": spot("seq", 1)},
        device_id_type=MESH,
    )
    rim_copy.start()
    gate_out[...] = (total[:, :width] * inv_rms).astype(jnp.bfloat16)
    chan_out[...] = (total[:, width:] * inv_rms).astype(jnp.bfloat16)
    step_out[...] = total_step[...] * inv_rms
    rim_copy.wait()
    rim_out[...] = rim_land[...]


def project(tokens, w_inner, w_group, w_step, pre_gain):
    rows, feat = tokens.shape
    depth, _, width = w_inner.shape
    heads = w_step.shape[1]
    state = w_group.shape[3]
    blocks = depth // feat
    columns = 2 * width + 2 * state
    vmem = pl.BlockSpec(memory_space=pltpu.VMEM)
    anywhere = pl.BlockSpec(memory_space=pl.ANY)
    return pl.pallas_call(
        project_kernel,
        out_shape=[
            jax.ShapeDtypeStruct((rows, width), jnp.bfloat16),
            jax.ShapeDtypeStruct((rows, width + 2 * state), jnp.bfloat16),
            jax.ShapeDtypeStruct((rows, heads), jnp.float32),
            jax.ShapeDtypeStruct((16, width + 2 * state), jnp.bfloat16),
        ],
        in_specs=[anywhere, anywhere, anywhere, vmem, vmem],
        out_specs=[vmem] * 4,
        scratch_shapes=[
            pltpu.VMEM((2 * depth, width), jnp.bfloat16),
            pltpu.VMEM((4 * depth, state), jnp.bfloat16),
            pltpu.VMEM((depth, columns), jnp.bfloat16),
            pltpu.VMEM((width // 128, 2 * CHUNK, 128), jnp.float32),
            pltpu.VMEM((4 * CHUNK, 128), jnp.float32),
            pltpu.VMEM((blocks, rows, feat), jnp.bfloat16),
            pltpu.VMEM((rows, columns), jnp.float32),
            pltpu.VMEM((rows, heads), jnp.float32),
            pltpu.VMEM((rows, 128), jnp.float32),
            pltpu.SemaphoreType.DMA((2, PARTS)),
            pltpu.SemaphoreType.DMA,
            pltpu.SemaphoreType.DMA((2, 20)),
            pltpu.SemaphoreType.DMA((2, 20)),
            pltpu.VMEM((16, width + 2 * state), jnp.bfloat16),
            pltpu.VMEM((16, width + 2 * state), jnp.bfloat16),
            pltpu.SemaphoreType.DMA((2,)),
        ],
        compiler_params=pltpu.CompilerParams(
            collective_id=0, has_side_effects=True, vmem_limit_bytes=VMEM_LIMIT
        ),
        name="project",
    )(tokens, w_inner, w_group, w_step.T, pre_gain[None, :])


NEVER = -1e30


def spans(lengths, deal):
    found = []
    begin = 0
    for k in range(lengths.shape[0]):
        end = begin + lengths[k]
        found.append((begin, end, deal[k]))
        begin = end
    return found


def head_column(values):
    heads = values.shape[0]
    places = lax.broadcasted_iota(jnp.int32, (heads, 1), 0)
    column = jnp.zeros((heads, 1), jnp.float32)
    for h in range(heads):
        column = jnp.where(places == h, values[h], column)
    return column


def by_head(tile, size):
    heads, width = tile.shape
    return jnp.reshape(
        jnp.broadcast_to(tile[:, None, :], (heads, size, width)), (heads * size, width)
    )


def columns_of(rows_by_head, count):
    heads = rows_by_head.shape[0]
    padding = jnp.zeros((128 - heads, count), jnp.float32)
    return jnp.concatenate([rows_by_head, padding], axis=0).T


def scan_kernel(
    lengths,
    deal,
    step_bias,
    decay_log,
    skip,
    chan,
    rim,
    step_raw,
    taps,
    bias,
    edges,
    init_states,
    partial_y,
    mixed,
    decay_column,
    decay_row,
    step_row,
    reach_column,
    carry_column,
    state_out,
    gain_out,
    finals_out,
    factor_out,
    longer,
    init,
    square,
    turned,
    states,
    factors,
    init_dot,
    load_sem,
):
    rows, width = chan.shape
    heads = step_raw.shape[1]
    requests = lengths.shape[0]
    inner = partial_y.shape[1]
    size = inner // heads
    state = (width - inner) // 2
    kernel = taps.shape[0]
    load = pltpu.make_async_copy(init_states, init, load_sem)
    load.start()
    first_row = lax.axis_index("seq") * rows
    places = spans(lengths, deal)

    def layout(shape, dim):
        local = lax.broadcasted_iota(jnp.int32, shape, dim)
        position = local + first_row
        start = jnp.zeros(shape, jnp.int32)
        owner = jnp.zeros(shape, jnp.int32)
        for begin, _, slot in places:
            started = position >= begin
            start = jnp.where(started, begin, start)
            owner = jnp.where(started, slot, owner)
        return local, position, position - start, owner

    local_c, position_c, offset_c, owner_c = layout((rows, 1), 0)
    local_r, _, offset_r, _ = layout((1, rows), 1)
    within_c = lax.rem(local_c, BLOCK)
    within_r = lax.rem(local_r, BLOCK)
    reach_c = jnp.minimum(offset_c, within_c)
    reach_r = jnp.minimum(offset_r, within_r)
    flag_c = offset_c > within_c
    flag_r = offset_r > within_r
    reach_column[...] = reach_c

    square[...] = jnp.zeros_like(square)
    square[:, :heads] = step_raw[...]
    raw_row = square[...].T[:heads] + head_column(step_bias)
    step = jnp.maximum(raw_row, 0.0) + jnp.log1p(jnp.exp(-jnp.abs(raw_row)))
    run = -jnp.exp(head_column(decay_log)) * step
    shift = 1
    while shift < BLOCK:
        run = run + jnp.where(reach_r >= shift, pltpu.roll(run, shift, 1), 0.0)
        shift *= 2
    run_c = columns_of(run, rows)
    step_row[...] = step
    decay_row[...] = run
    decay_column[...] = run_c
    coef_c = jnp.exp(run_c)
    carry_c = jnp.where(flag_c, coef_c, 0.0)
    init_c = jnp.where(flag_c, 0.0, coef_c)
    carry_column[0:BLOCK, :] = carry_c[0:BLOCK]
    carry_column[BLOCK:, :] = carry_c[BLOCK:] * carry_c[BLOCK - 1 : BLOCK, :]

    longer[0:8, :] = rim[8:16, :].astype(jnp.float32)
    longer[8:, :] = chan[...].astype(jnp.float32)
    summed = bias[...] + taps[kernel - 1 : kernel, :] * longer[8:, :]
    choices = lax.broadcasted_iota(jnp.int32, (rows, edges.shape[0]), 1)
    for back in range(1, kernel):
        slot = (kernel - 1 - back + offset_c) * requests + owner_c
        lookup = ((choices == slot) & (offset_c < back)).astype(jnp.float32).astype(jnp.bfloat16)
        from_edge = jnp.dot(lookup, edges[...], preferred_element_type=jnp.float32)
        value = jnp.where(offset_c >= back, longer[8 - back : 8 - back + rows, :], from_edge)
        summed = summed + taps[kernel - 1 - back : kernel - back, :] * value
    mixed[...] = (summed * (1.0 / (1.0 + jnp.exp(-summed)))).astype(jnp.bfloat16)
    turned[...] = mixed[:, :inner].astype(jnp.float32).T.astype(jnp.bfloat16)
    states[...] = jnp.zeros_like(states)
    factors[...] = jnp.zeros_like(factors)
    init_dot[...] = jnp.zeros_like(init_dot)
    load.wait()

    def pick(values, at):
        return jnp.sum(jnp.where(local_r == at, values, jnp.zeros_like(values)), axis=1, keepdims=True)

    def emit(at, index, slot):
        reach = pick(reach_r, at)
        flagged = pick(flag_r.astype(jnp.int32), at) > 0
        run_at = pick(run, at)
        keep = (local_r <= at) & (local_r >= at - reach)
        share = jnp.exp(jnp.where(keep, run_at - run, NEVER)) * step
        share = share.astype(jnp.bfloat16).astype(jnp.float32)
        spread = (turned[...].astype(jnp.float32) * by_head(share, size)).astype(jnp.bfloat16)
        value = jnp.dot(spread, mixed[:, inner : inner + state], preferred_element_type=jnp.float32)
        coef = jnp.exp(run_at)
        carry = jnp.broadcast_to(jnp.where(flagged, coef, 0.0), (heads, state))
        start = jnp.broadcast_to(jnp.where(flagged, 0.0, coef), (heads, state))
        late = at >= BLOCK
        first_gain = jnp.broadcast_to(
            jnp.where(pick(flag_r.astype(jnp.int32), BLOCK - 1) > 0, jnp.exp(pick(run, BLOCK - 1)), 0.0),
            (heads, state),
        )
        value = value + by_head(start, size) * init[slot]
        value = value + by_head(jnp.where(late, carry, 0.0), size) * states[0]
        states[index] = value
        factors[index] = carry * jnp.where(late, first_gain, 1.0)

    def request(k, begin):
        end = begin + lengths[k]
        slot = deal[k]
        low = begin - first_row
        high = end - first_row

        @pl.when((high > 0) & (low < rows))
        def _():
            chosen = (local_c >= low) & (local_c < high) & jnp.logical_not(flag_c)
            picked = jnp.where(chosen, mixed[:, inner + state :].astype(jnp.float32), 0.0)
            init_dot[...] += lax.dot_general(
                picked.astype(jnp.bfloat16),
                init[slot].astype(jnp.bfloat16),
                (((1,), (1,)), ((), ())),
                preferred_element_type=jnp.float32,
            )

            def place(j, carry):
                at = jnp.where(j < 2, BLOCK - 1 + j * BLOCK, high - 1)
                index = jnp.where(j < 2, j, 2 + slot)

                @pl.when((at >= low) & (at < high) & (at >= 0) & (at < rows))
                def _():
                    emit(at, index, slot)

                return carry

            lax.fori_loop(0, 3, place, 0)

        return end

    lax.fori_loop(0, requests, request, jnp.int32(0))
    state_out[...] = states[1].astype(jnp.bfloat16)
    gain_out[...] = factors[1]
    finals_out[...] = states[2:].astype(jnp.bfloat16)
    factor_out[...] = factors[2:]
    carried = lax.dot_general(
        mixed[BLOCK:, inner + state :],
        states[0].astype(jnp.bfloat16),
        (((1,), (1,)), ((), ())),
        preferred_element_type=jnp.float32,
    )
    for h in range(heads):
        span = slice(h * size, (h + 1) * size)
        value = skip[h] * mixed[:, span].astype(jnp.float32)
        value = value + init_c[:, h : h + 1] * init_dot[:, span]
        partial_y[0:BLOCK, span] = value[0:BLOCK]
        partial_y[BLOCK:, span] = value[BLOCK:] + carry_c[BLOCK:, h : h + 1] * carried[:, span]


def scan(
    lengths, deal, step_bias, decay_log, skip, chan, rim, step_raw, taps, bias, edges, init_states
):
    rows, width = chan.shape
    heads = step_raw.shape[1]
    requests, _, size, state = init_states.shape
    inner = heads * size
    smem = pl.BlockSpec(memory_space=pltpu.SMEM)
    vmem = pl.BlockSpec(memory_space=pltpu.VMEM)
    anywhere = pl.BlockSpec(memory_space=pl.ANY)
    f32, bf = jnp.float32, jnp.bfloat16
    shape = jax.ShapeDtypeStruct
    return pl.pallas_call(
        scan_kernel,
        out_shape=[
            shape((rows, inner), f32),
            shape((rows, width), bf),
            shape((rows, 128), f32),
            shape((heads, rows), f32),
            shape((heads, rows), f32),
            shape((rows, 1), jnp.int32),
            shape((rows, 128), f32),
            shape((inner, state), bf),
            shape((heads, state), f32),
            shape((requests, inner, state), bf),
            shape((requests, heads, state), f32),
        ],
        in_specs=[smem] * 5 + [vmem] * 6 + [anywhere],
        out_specs=[vmem] * 11,
        scratch_shapes=[
            pltpu.VMEM((rows + 8, width), f32),
            pltpu.VMEM((requests, inner, state), f32),
            pltpu.VMEM((rows, 128), f32),
            pltpu.VMEM((inner, rows), bf),
            pltpu.VMEM((requests + 2, inner, state), f32),
            pltpu.VMEM((requests + 2, heads, state), f32),
            pltpu.VMEM((rows, inner), f32),
            pltpu.SemaphoreType.DMA,
        ],
        compiler_params=pltpu.CompilerParams(vmem_limit_bytes=VMEM_LIMIT),
        name="scan",
    )(
        lengths,
        deal,
        step_bias,
        decay_log,
        skip,
        chan,
        rim,
        step_raw,
        taps,
        bias,
        edges,
        jnp.reshape(init_states, (requests, inner, state)),
    )


def slot_ends(lengths, deal, first_row, shape, dim):
    requests = lengths.shape[0]
    slots = lax.broadcasted_iota(jnp.int32, shape, dim)
    ends = jnp.zeros(shape, jnp.int32)
    end = -1 - first_row
    for k in range(requests):
        end = end + lengths[k]
        ends = jnp.where(slots == deal[k], end, ends)
    return ends


def finish_kernel(
    lengths,
    deal,
    partial_y,
    mixed,
    decay_column,
    decay_row,
    step_row,
    reach_column,
    carry_column,
    state_own,
    gain_own,
    finals_own,
    factor_own,
    gate_in,
    inner_gain,
    w_out,
    tokens,
    w_head,
    final_gain,
    hidden,
    final_states,
    logits,
    weights,
    head,
    partials,
    stage_far,
    stage_near,
    land_far,
    land_near,
    stage_far2,
    stage_near2,
    land_far2,
    land_near2,
    picks,
    rows_all,
    wide_rows,
    load_sem,
    sends,
    recvs,
    pick_sends,
    pick_recvs,
    row_sends,
    row_recvs,
    outputs,
    normed,
    scales,
    entry_held,
    land_state,
    land_gain,
    square_own,
    square_land,
    outbox,
    pair_land,
    pair_sum,
    final_land,
    far_sends,
    far_recvs,
):
    rows, feat = tokens.shape
    heads, inner = decay_row.shape[0], gate_in.shape[1]
    size = inner // heads
    state = state_own.shape[1]
    requests = lengths.shape[0]
    seq = lax.axis_size("seq")
    load_out = pltpu.make_async_copy(w_out, weights, load_sem.at[0])
    load_head = pltpu.make_async_copy(w_head, head, load_sem.at[1])
    load_out.start()
    load_head.start()
    plane = [(dr, dc) for dr in range(4) for dc in range(4) if dr or dc]
    peers = [{axis: spot(axis, shift)} for axis, shift in PLANE]
    peers += [{"seq": spot("seq", shift)} for shift in range(1, seq)]
    peers += [
        {"row": spot("row", dr), "col": spot("col", dc)}
        for dr, dc in plane
        if not ((dr == 0 and dc != 2) or (dc == 0 and dr != 2))
    ]
    greet(peers)
    extra = []

    def hand(src, dst, number, place):
        copy = pltpu.make_async_remote_copy(
            src_ref=src,
            dst_ref=dst,
            send_sem=far_sends.at[number],
            recv_sem=far_recvs.at[number],
            device_id=place,
            device_id_type=MESH,
        )
        copy.start()
        extra.append(copy)
        return copy

    hand(state_own, land_state.at[0], 0, {"seq": spot("seq", 1)})
    hand(gain_own, land_gain, 1, {"seq": spot("seq", 1)})
    hand(state_own, land_state.at[1], 2, {"seq": spot("seq", 2)})

    def inside(b, carry):
        place = pl.ds(pl.multiple_of(b * BLOCK, BLOCK), BLOCK)
        scores = lax.dot_general(
            mixed[place, inner + state :],
            mixed[place, inner : inner + state],
            (((1,), (1,)), ((), ())),
            preferred_element_type=jnp.float32,
        )
        target = lax.broadcasted_iota(jnp.int32, (BLOCK, BLOCK), 0)
        source = lax.broadcasted_iota(jnp.int32, (BLOCK, BLOCK), 1)
        keep = (source <= target) & (source >= target - reach_column[place, :])
        for h in range(heads):
            span = slice(h * size, (h + 1) * size)
            diff = decay_column[place, h : h + 1] - decay_row[h : h + 1, place]
            decay = jnp.exp(jnp.where(keep, diff, NEVER))
            weight = (scores * decay * step_row[h : h + 1, place]).astype(jnp.bfloat16)
            outputs[place, span] = partial_y[place, span] + jnp.dot(
                weight, mixed[place, span], preferred_element_type=jnp.float32
            )
        return carry

    lax.fori_loop(0, rows // BLOCK, inside, 0)
    for copy in extra:
        copy.wait_recv()
    entry = land_state[0].astype(jnp.float32) + by_head(land_gain[...], size) * land_state[
        1
    ].astype(jnp.float32)
    entry_held[...] = entry
    carried = lax.dot_general(
        mixed[:, inner + state :],
        entry.astype(jnp.bfloat16),
        (((1,), (1,)), ((), ())),
        preferred_element_type=jnp.float32,
    )
    squares = jnp.zeros((rows, 128), jnp.float32)
    left = lax.broadcasted_iota(jnp.int32, (rows, 128), 1) < size
    for tile in range(inner // 128):
        span = slice(tile * 128, (tile + 1) * 128)
        coef = jnp.where(
            left, carry_column[:, 2 * tile : 2 * tile + 1], carry_column[:, 2 * tile + 1 : 2 * tile + 2]
        )
        gate = gate_in[:, span].astype(jnp.float32)
        gated = (outputs[:, span] + coef * carried[:, span]) * (gate / (1.0 + jnp.exp(-gate)))
        squares = squares + gated * gated
        normed[:, span] = (gated * inner_gain[:, span]).astype(jnp.bfloat16)
    square_own[...] = jnp.broadcast_to(
        jnp.sum(squares.T, axis=0, keepdims=True), square_own.shape
    )
    partner = lax.axis_index("col") + 1 - 2 * lax.rem(lax.axis_index("col"), 2)
    square_copy = hand(square_own, square_land, 3, {"col": partner})
    load_out.wait()

    def compute(first, count, scale=None):
        def body(i, carry):
            half = lax.rem(i, 2)
            j = i // 2 + first
            dv = 2 - j // 4 - j // 8 + (j // 12) * 2
            du = 2 - lax.rem(j, 4) - lax.rem(j, 4) // 2 + (lax.rem(j, 4) // 3) * 2
            block = block_of(half, du, dv)
            place = pl.ds(pl.multiple_of(half * HALF, HALF), HALF)
            value = jnp.dot(
                normed[place, :],
                weights[:, pl.ds(pl.multiple_of(block * feat, feat), feat)],
                preferred_element_type=jnp.float32,
            )
            if scale is not None:
                value = value * scale[place, :]
            partials[half, j] = value
            return carry

        lax.fori_loop(0, 2 * count, body, 0)

    started = {}

    def send(half, number, src, dst, axis, shift):
        copy = remote(src, dst, sends.at[half], recvs.at[half], number, axis, shift)
        copy.start()
        started[half, number] = copy

    def far(half, values, stage, land, number, axis):
        for side in (0, 1):
            stage[side] = values[side * 128 : side * 128 + 128].astype(jnp.bfloat16)
            send(half, number + side, stage.at[side], land.at[side], axis, 1 - 2 * side)

    def near(half, side, values, far_land, far_number, stage, land, number, axis):
        started[half, far_number + side].wait_recv()
        extra = far_land[side].astype(jnp.float32)
        keep = slice(128 - 128 * side, 256 - 128 * side)
        mix = slice(128 * side, 128 * side + 128)
        stage[side, mix] = (values[mix] + extra).astype(jnp.bfloat16)
        stage[side, keep] = values[keep].astype(jnp.bfloat16)
        send(half, number + side, stage.at[side], land.at[side], axis, 1 - 2 * side)

    compute(0, 4)
    square_copy.wait_recv()
    both = square_own[0:1, :] + square_land[0:1, :]
    scale_row = lax.rsqrt(both / (2 * inner) + EPSILON)
    scale_tile = jnp.broadcast_to(scale_row, (128, rows)).T
    scales[...] = jnp.concatenate([scale_tile, scale_tile], axis=1)
    for k in range(4):
        for half in (0, 1):
            far(
                half,
                partials[half, k] * scales[half * HALF : half * HALF + HALF, :],
                stage_far.at[half, k],
                land_far.at[half, k],
                2 * k,
                AXES[half][1],
            )
    compute(4, 12, scales)
    core = lax.rem(lax.axis_index("seq"), 2)
    chip = lax.axis_index("seq") // 2
    chips = seq // 2

    def fill(o, carry):
        value = finals_own[o].astype(jnp.float32) + by_head(factor_own[o], size) * entry_held[...]
        outbox[lax.rem(o // 2, 2), o // 4, lax.rem(o, 2)] = value.astype(jnp.bfloat16)
        return carry

    lax.fori_loop(0, requests, fill, 0)
    pair_copy = hand(outbox.at[1 - core], pair_land, 4, {"seq": spot("seq", 1 - 2 * core)})
    for k in range(4):
        for half in (0, 1):
            for side in (0, 1):
                near(
                    half,
                    side,
                    partials[half, 4 + 4 * side + k],
                    land_far.at[half, k],
                    2 * k,
                    stage_near.at[half, k],
                    land_near.at[half, k],
                    8 + 2 * k,
                    AXES[half][1],
                )
    pair_copy.wait_recv()
    for d in range(chips):
        there = lax.rem(chip + d, chips)
        pair_sum[d] = (
            outbox[core, there].astype(jnp.float32) + pair_land[there].astype(jnp.float32)
        ).astype(jnp.bfloat16)
    final_copies = [
        hand(pair_sum.at[d], final_land.at[d - 1], 4 + d, {"seq": spot("seq", 2 * d)})
        for d in range(1, chips)
    ]
    for k in range(4):
        for half in (0, 1):
            axis = AXES[half][0]
            total = partials[half, 12 + k]
            for side in (0, 1):
                started[half, 8 + 2 * k + side].wait_recv()
                total = total + land_near[half, k, side].astype(jnp.float32)
            if k == 0:
                far(half, total, stage_far2.at[half], land_far2.at[half], 16, axis)
            elif k < 3:
                near(
                    half,
                    k - 1,
                    total,
                    land_far2.at[half],
                    16,
                    stage_near2.at[half],
                    land_near2.at[half],
                    18,
                    axis,
                )
            else:
                for side in (0, 1):
                    started[half, 18 + side].wait_recv()
                    total = total + land_near2[half, side].astype(jnp.float32)
                place = slice(half * HALF, half * HALF + HALF)
                hidden[place, :] = (tokens[place, :].astype(jnp.float32) + total).astype(
                    jnp.bfloat16
                )
    first_row = lax.axis_index("seq") * rows
    ends = slot_ends(lengths, deal, first_row, (requests, rows), 0)
    chooser = (ends == lax.broadcasted_iota(jnp.int32, (requests, rows), 1)).astype(jnp.bfloat16)
    picks[0] = jnp.dot(chooser, hidden[...], preferred_element_type=jnp.float32).astype(
        jnp.bfloat16
    )
    handed = []
    for shift in range(1, seq):
        copy = remote(
            picks.at[0], picks.at[shift], pick_sends, pick_recvs, shift, "seq", shift
        )
        copy.start()
        handed.append(copy)
    for copy in handed:
        copy.wait_recv()
    whole = picks[0].astype(jnp.float32)
    for shift in range(1, seq):
        whole = whole + picks[shift].astype(jnp.float32)
    own = block_of(0, 0, 0)
    rows_all[own] = whole.astype(jnp.bfloat16)
    for number, (dr, dc) in enumerate(plane):
        copy = pltpu.make_async_remote_copy(
            src_ref=rows_all.at[own],
            dst_ref=rows_all.at[own],
            send_sem=row_sends.at[number],
            recv_sem=row_recvs.at[number],
            device_id={"row": spot("row", dr), "col": spot("col", dc)},
            device_id_type=MESH,
        )
        copy.start()
        handed.append(copy)
    for copy in handed[seq - 1 :]:
        copy.wait_recv()
    for copy in final_copies:
        copy.wait_recv()
    final = pair_sum[0].astype(jnp.float32)
    for d in range(1, chips):
        final = final + final_land[d - 1].astype(jnp.float32)
    final_states[...] = final
    load_head.wait()
    total = jnp.zeros((requests, 128), jnp.float32)
    for block in range(len(plane) + 1):
        value = rows_all[block].astype(jnp.float32)
        wide_rows[:, block * feat : (block + 1) * feat] = value
        total = total + value[:, :128] * value[:, :128] + value[:, 128:] * value[:, 128:]
    depth = w_head.shape[0]
    scale = lax.rsqrt(jnp.sum(total, axis=1, keepdims=True) / depth + EPSILON)
    head_in = (wide_rows[...] * scale * final_gain[...]).astype(jnp.bfloat16)
    logits[...] = jnp.dot(head_in, head[...], preferred_element_type=jnp.float32)
    for copy in handed:
        copy.wait_send()
    for copy in list(started.values()) + extra:
        copy.wait_send()


def finish(lengths, deal, arrays, gate_in, inner_gain, w_out, tokens, w_head, final_gain):
    rows, feat = tokens.shape
    inner, depth = w_out.shape
    requests = lengths.shape[0]
    vocab = w_head.shape[1]
    seq = lax.axis_size("seq")
    state = arrays[7].shape[1]
    heads = arrays[8].shape[0]
    slots = requests // seq
    smem = pl.BlockSpec(memory_space=pltpu.SMEM)
    vmem = pl.BlockSpec(memory_space=pltpu.VMEM)
    anywhere = pl.BlockSpec(memory_space=pl.ANY)
    bf, f32 = jnp.bfloat16, jnp.float32
    return pl.pallas_call(
        finish_kernel,
        out_shape=[
            jax.ShapeDtypeStruct((rows, feat), bf),
            jax.ShapeDtypeStruct((slots, inner, state), f32),
            jax.ShapeDtypeStruct((requests, vocab), f32),
        ],
        in_specs=[smem, smem] + [vmem] * 13 + [anywhere, vmem, anywhere, vmem],
        out_specs=[vmem] * 3,
        scratch_shapes=[
            pltpu.VMEM((inner, depth), bf),
            pltpu.VMEM((depth, vocab), bf),
            pltpu.VMEM((2, 16, HALF, feat), f32),
            pltpu.VMEM((2, 4, 2, 128, feat), bf),
            pltpu.VMEM((2, 4, 2, 256, feat), bf),
            pltpu.VMEM((2, 4, 2, 128, feat), bf),
            pltpu.VMEM((2, 4, 2, 256, feat), bf),
            pltpu.VMEM((2, 2, 128, feat), bf),
            pltpu.VMEM((2, 2, 256, feat), bf),
            pltpu.VMEM((2, 2, 128, feat), bf),
            pltpu.VMEM((2, 2, 256, feat), bf),
            pltpu.VMEM((seq, requests, feat), bf),
            pltpu.VMEM((16, requests, feat), bf),
            pltpu.VMEM((requests, depth), f32),
            pltpu.SemaphoreType.DMA((2,)),
            pltpu.SemaphoreType.DMA((2, 20)),
            pltpu.SemaphoreType.DMA((2, 20)),
            pltpu.SemaphoreType.DMA((seq,)),
            pltpu.SemaphoreType.DMA((seq,)),
            pltpu.SemaphoreType.DMA((15,)),
            pltpu.SemaphoreType.DMA((15,)),
            pltpu.VMEM((rows, inner), f32),
            pltpu.VMEM((rows, inner), bf),
            pltpu.VMEM((rows, feat), f32),
            pltpu.VMEM((inner, state), f32),
            pltpu.VMEM((2, inner, state), bf),
            pltpu.VMEM((heads, state), f32),
            pltpu.VMEM((8, rows), f32),
            pltpu.VMEM((8, rows), f32),
            pltpu.VMEM((2, seq // 2, slots, inner, state), bf),
            pltpu.VMEM((seq // 2, slots, inner, state), bf),
            pltpu.VMEM((seq // 2, slots, inner, state), bf),
            pltpu.VMEM((seq // 2 - 1, slots, inner, state), bf),
            pltpu.SemaphoreType.DMA((8,)),
            pltpu.SemaphoreType.DMA((8,)),
        ],
        compiler_params=pltpu.CompilerParams(
            collective_id=1, has_side_effects=True, vmem_limit_bytes=VMEM_LIMIT
        ),
        name="finish",
    )(
        lengths,
        deal,
        *arrays,
        gate_in,
        inner_gain[None, :],
        w_out,
        tokens,
        w_head,
        final_gain[None, :],
    )


def per_device(
    tokens,
    lengths,
    deal,
    pre_gain,
    w_inner,
    w_group,
    w_step,
    conv_inner,
    conv_group,
    conv_bias_inner,
    conv_bias_group,
    edge_inner,
    edge_group,
    init_states,
    step_bias,
    decay_log,
    skip,
    inner_gain,
    w_out,
    final_gain,
    w_head,
):
    requests = lengths.shape[0]
    kernel, inner = conv_inner.shape
    state = w_group.shape[3]
    heads = w_step.shape[1]
    local = lax.axis_index("col") * w_group.shape[2] // lax.axis_size("col")

    def pick_group(table, axis):
        return lax.dynamic_index_in_dim(table, local, axis, keepdims=False)

    taps = jnp.concatenate(
        [conv_inner, jnp.reshape(pick_group(conv_group, 2), (kernel, 2 * state))], axis=1
    )
    bias = jnp.concatenate(
        [conv_bias_inner, jnp.reshape(pick_group(conv_bias_group, 1), (2 * state,))]
    )[None, :]
    edges = jnp.concatenate(
        [
            jnp.transpose(edge_inner, (1, 0, 2)),
            jnp.transpose(
                jnp.reshape(pick_group(edge_group, 3), (requests, kernel - 1, 2 * state)), (1, 0, 2)
            ),
        ],
        axis=2,
    )
    edges = jnp.reshape(edges, ((kernel - 1) * requests, inner + 2 * state))
    gate_in, chan, step_raw, rim = project(tokens, w_inner, w_group, w_step, pre_gain)
    arrays = scan(
        lengths, deal, step_bias, decay_log, skip, chan, rim, step_raw, taps, bias, edges, init_states
    )
    hidden_out, final_states, logits = finish(
        lengths, deal, arrays, gate_in, inner_gain, w_out, tokens, w_head, final_gain
    )
    final_states = jnp.reshape(
        final_states, (final_states.shape[0], heads, inner // heads, state)
    )
    return (hidden_out, final_states, logits)


def solution(mesh):
    in_specs = (
        P("seq", ("row", "col")),
        P(),
        P(),
        P(),
        P(None, None, ("row", "col")),
        P(None, None, "row", None),
        P(None, ("row", "col")),
        P(None, ("row", "col")),
        P(None, None, "row", None),
        P(("row", "col")),
        P(None, "row", None),
        P(None, None, ("row", "col")),
        P(None, None, None, "row", None),
        P(None, ("row", "col"), None, None),
        P(("row", "col")),
        P(("row", "col")),
        P(("row", "col")),
        P(("row", "col")),
        P(("row", "col"), None),
        P(),
        P(None, ("seq", "row", "col")),
    )
    out_specs = (
        P("seq", ("row", "col")),
        P("seq", ("row", "col"), None, None),
        P(None, ("seq", "row", "col")),
    )
    return jax.shard_map(
        per_device, mesh=mesh, in_specs=in_specs, out_specs=out_specs, check_vma=False
    )
```

```python
import jax
import jax.numpy as jnp
from jax import lax
from jax.experimental import pallas as pl
from jax.experimental.pallas import tpu as pltpu
from jax.sharding import PartitionSpec as P

BLOCK = 256


EPSILON = 1e-05


MESH = pl.DeviceIdType.MESH
HALF = 256
FEAT = 256
VMEM_LIMIT = 62 * 1024 * 1024


def spot(axis, shift):
    size = lax.axis_size(axis)
    return lax.rem(lax.axis_index(axis) + shift + size, size)


def block_of(half, du, dv):
    row = spot("row", dv + half * (du - dv))
    col = spot("col", du + half * (dv - du))
    return row * lax.axis_size("col") + col


def remote(src, dst, sends, recvs, place, axis, shift):
    return pltpu.make_async_remote_copy(
        src_ref=src,
        dst_ref=dst,
        send_sem=sends.at[place],
        recv_sem=recvs.at[place],
        device_id={axis: spot(axis, shift)},
        device_id_type=MESH,
    )


def greet(peers):
    barrier = pltpu.get_barrier_semaphore()
    for peer in peers:
        pl.semaphore_signal(barrier, inc=1, device_id=peer, device_id_type=MESH)
    pl.semaphore_wait(barrier, len(peers))


PLANE = (("row", 1), ("row", -1), ("col", 1), ("col", -1))
AXES = (("col", "row"), ("row", "col"))
ORDER = (0, -1, 1, 2)
CHUNK = 64
PARTS = 4


def project_kernel(
    tokens,
    w_inner,
    w_group,
    w_step,
    gain,
    gate_out,
    chan_out,
    step_out,
    rim_out,
    raw_inner,
    raw_group,
    weights,
    wide_inner,
    wide_group,
    held,
    total,
    total_step,
    squares,
    load_sem,
    own_sem,
    sends,
    recvs,
    rim_stage,
    rim_land,
    rim_sems,
):
    depth = weights.shape[0]
    width = gate_out.shape[1]
    lanes = 128
    rows_part = depth // PARTS
    flat_inner = w_inner.reshape(2 * depth, width)
    flat_group = w_group.reshape(4 * depth, lanes)
    loads = []
    for part in range(PARTS):
        loads.append(
            (
                pltpu.make_async_copy(
                    flat_inner.at[pl.ds(2 * rows_part * part, 2 * rows_part)],
                    raw_inner.at[pl.ds(2 * rows_part * part, 2 * rows_part)],
                    load_sem.at[0, part],
                ),
                pltpu.make_async_copy(
                    flat_group.at[pl.ds(4 * rows_part * part, 4 * rows_part)],
                    raw_group.at[pl.ds(4 * rows_part * part, 4 * rows_part)],
                    load_sem.at[1, part],
                ),
            )
        )
    for part in range(PARTS):
        loads[part][0].start()
        loads[part][1].start()
    own = block_of(0, 0, 0)
    own_copy = pltpu.make_async_copy(tokens, held.at[own], own_sem)
    own_copy.start()
    greet([{axis: spot(axis, shift)} for axis, shift in PLANE + (("seq", 1), ("seq", -1))])
    messages = {}

    def send(half, number, du, dv, axis, shift, first, count, from_own=False):
        block = block_of(half, du, dv)
        rows = pl.ds(half * HALF + first, count)
        src = tokens.at[rows] if from_own else held.at[block, rows]
        copy = remote(
            src, held.at[block, rows], sends.at[half], recvs.at[half], number, axis, shift
        )
        copy.start()
        messages[half, number] = copy

    def arrive(half, *numbers):
        for number in numbers:
            messages[half, number].wait_recv()

    def spread(half, k, from_own=False):
        axis = AXES[half][1]
        send(half, 4 + 4 * k, ORDER[k], 0, axis, 1, 0, HALF, from_own)
        send(half, 5 + 4 * k, ORDER[k], 0, axis, -1, 0, HALF, from_own)

    def relay(half, k):
        axis = AXES[half][1]
        arrive(half, 4 + 4 * k)
        send(half, 6 + 4 * k, ORDER[k], -1, axis, 1, 0, HALF // 2)
        arrive(half, 5 + 4 * k)
        send(half, 7 + 4 * k, ORDER[k], 1, axis, -1, HALF // 2, HALF // 2)

    for half in (0, 1):
        axis = AXES[half][0]
        send(half, 0, 0, 0, axis, 1, 0, HALF, True)
        send(half, 1, 0, 0, axis, -1, 0, HALF, True)
    for half in (0, 1):
        spread(half, 0, True)
    group_local = lax.axis_index("col") * 2 // lax.axis_size("col")

    def untangle(part):
        loads[part][0].wait()
        loads[part][1].wait()

        def body(i, carry):
            base = pl.multiple_of(part * rows_part + i * CHUNK, CHUNK)
            for j in range(width // lanes):
                wide_inner[j] = raw_inner[
                    pl.ds(2 * base, 2 * CHUNK), j * lanes : (j + 1) * lanes
                ].astype(jnp.float32)
            wide_group[...] = raw_group[pl.ds(4 * base, 4 * CHUNK), :].astype(jnp.float32)
            for which in range(2):
                for j in range(width // lanes):
                    weights[
                        pl.ds(base, CHUNK), which * width + j * lanes : which * width + (j + 1) * lanes
                    ] = wide_inner[j, pl.ds(which, CHUNK, stride=2), :].astype(jnp.bfloat16)
                start = 2 * width + which * lanes
                weights[pl.ds(base, CHUNK), start : start + lanes] = wide_group[
                    pl.ds(2 * which + group_local, CHUNK, stride=4), :
                ].astype(jnp.bfloat16)
            return carry

        lax.fori_loop(0, rows_part // CHUNK, body, 0)

    total[...] = jnp.zeros_like(total)
    total_step[...] = jnp.zeros_like(total_step)
    squares[...] = jnp.zeros_like(squares)

    def multiply(half, du, dv):
        block = block_of(half, du, dv)
        rows = pl.ds(pl.multiple_of(half * HALF, HALF), HALF)
        column = pl.multiple_of(block * FEAT, FEAT)
        wide = held[block, rows, :].astype(jnp.float32)
        squares[rows, :] += wide[:, :lanes] * wide[:, :lanes] + wide[:, lanes:] * wide[:, lanes:]
        scaled = (wide * gain[:, pl.ds(column, FEAT)]).astype(jnp.bfloat16)
        total[rows, :] += jnp.dot(
            scaled, weights[pl.ds(column, FEAT), :], preferred_element_type=jnp.float32
        )
        total_step[rows, :] += lax.dot_general(
            scaled,
            w_step[:, pl.ds(column, FEAT)],
            (((1,), (1,)), ((), ())),
            preferred_element_type=jnp.float32,
        )

    def run(count, pick):
        def body(i, carry):
            half = lax.rem(i, 2)
            du, dv = pick(i // 2)
            multiply(half, du, dv)
            return carry

        lax.fori_loop(0, 2 * count, body, 0)

    untangle(0)
    for half in (0, 1):
        arrive(half, 0)
        send(half, 2, -1, 0, AXES[half][0], 1, 0, HALF // 2)
        spread(half, 1)
        arrive(half, 1)
        send(half, 3, 1, 0, AXES[half][0], -1, HALF // 2, HALF // 2)
        spread(half, 2)
    untangle(1)
    for half in (0, 1):
        relay(half, 0)
    untangle(2)
    for half in (0, 1):
        arrive(half, 2, 3)
        spread(half, 3)
    untangle(3)
    own_copy.wait()
    run(2, lambda j: (j, 0))
    for half in (0, 1):
        relay(half, 1)
    run(2, lambda j: (j + 2, 0))
    for half in (0, 1):
        relay(half, 2)
    run(4, lambda j: (-(j // 2), 2 * lax.rem(j, 2) - 1))
    for half in (0, 1):
        relay(half, 3)
    run(4, lambda j: (1 + j // 2, 2 * lax.rem(j, 2) - 1))
    for k in range(4):
        for half in (0, 1):
            arrive(half, 6 + 4 * k, 7 + 4 * k)
        run(1, lambda j: (ORDER[k], 2))
    for half in (0, 1):
        for number in range(20):
            messages[half, number].wait_send()
    inv_rms = lax.rsqrt(jnp.sum(squares[...], axis=1, keepdims=True) / depth + EPSILON)
    last = total.shape[0] - rim_stage.shape[0]
    rim_stage[...] = (total[last:, width:] * inv_rms[last:]).astype(jnp.bfloat16)
    rim_copy = pltpu.make_async_remote_copy(
        src_ref=rim_stage,
        dst_ref=rim_land,
        send_sem=rim_sems.at[0],
        recv_sem=rim_sems.at[1],
        device_id={"seq": spot("seq", 1)},
        device_id_type=MESH,
    )
    rim_copy.start()
    gate_out[...] = (total[:, :width] * inv_rms).astype(jnp.bfloat16)
    chan_out[...] = (total[:, width:] * inv_rms).astype(jnp.bfloat16)
    step_out[...] = total_step[...] * inv_rms
    rim_copy.wait()
    rim_out[...] = rim_land[...]


def project(tokens, w_inner, w_group, w_step, pre_gain):
    rows, feat = tokens.shape
    depth, _, width = w_inner.shape
    heads = w_step.shape[1]
    state = w_group.shape[3]
    blocks = depth // feat
    columns = 2 * width + 2 * state
    vmem = pl.BlockSpec(memory_space=pltpu.VMEM)
    anywhere = pl.BlockSpec(memory_space=pl.ANY)
    return pl.pallas_call(
        project_kernel,
        out_shape=[
            jax.ShapeDtypeStruct((rows, width), jnp.bfloat16),
            jax.ShapeDtypeStruct((rows, width + 2 * state), jnp.bfloat16),
            jax.ShapeDtypeStruct((rows, heads), jnp.float32),
            jax.ShapeDtypeStruct((16, width + 2 * state), jnp.bfloat16),
        ],
        in_specs=[anywhere, anywhere, anywhere, vmem, vmem],
        out_specs=[vmem] * 4,
        scratch_shapes=[
            pltpu.VMEM((2 * depth, width), jnp.bfloat16),
            pltpu.VMEM((4 * depth, state), jnp.bfloat16),
            pltpu.VMEM((depth, columns), jnp.bfloat16),
            pltpu.VMEM((width // 128, 2 * CHUNK, 128), jnp.float32),
            pltpu.VMEM((4 * CHUNK, 128), jnp.float32),
            pltpu.VMEM((blocks, rows, feat), jnp.bfloat16),
            pltpu.VMEM((rows, columns), jnp.float32),
            pltpu.VMEM((rows, heads), jnp.float32),
            pltpu.VMEM((rows, 128), jnp.float32),
            pltpu.SemaphoreType.DMA((2, PARTS)),
            pltpu.SemaphoreType.DMA,
            pltpu.SemaphoreType.DMA((2, 20)),
            pltpu.SemaphoreType.DMA((2, 20)),
            pltpu.VMEM((16, width + 2 * state), jnp.bfloat16),
            pltpu.VMEM((16, width + 2 * state), jnp.bfloat16),
            pltpu.SemaphoreType.DMA((2,)),
        ],
        compiler_params=pltpu.CompilerParams(
            collective_id=0, has_side_effects=True, vmem_limit_bytes=VMEM_LIMIT
        ),
        name="project",
    )(tokens, w_inner, w_group, w_step.T, pre_gain[None, :])


NEVER = -1e30


def spans(lengths, deal):
    found = []
    begin = 0
    for k in range(lengths.shape[0]):
        end = begin + lengths[k]
        found.append((begin, end, deal[k]))
        begin = end
    return found


def head_column(values):
    heads = values.shape[0]
    places = lax.broadcasted_iota(jnp.int32, (heads, 1), 0)
    column = jnp.zeros((heads, 1), jnp.float32)
    for h in range(heads):
        column = jnp.where(places == h, values[h], column)
    return column


def by_head(tile, size):
    heads, width = tile.shape
    return jnp.reshape(
        jnp.broadcast_to(tile[:, None, :], (heads, size, width)), (heads * size, width)
    )


def columns_of(rows_by_head, count):
    heads = rows_by_head.shape[0]
    padding = jnp.zeros((128 - heads, count), jnp.float32)
    return jnp.concatenate([rows_by_head, padding], axis=0).T


def scan_kernel(
    lengths,
    deal,
    step_bias,
    decay_log,
    skip,
    chan,
    rim,
    step_raw,
    conv_inner,
    conv_group,
    bias_inner,
    bias_group,
    edge_inner,
    edge_group,
    init_states,
    partial_y,
    mixed,
    decay_column,
    decay_row,
    step_row,
    reach_column,
    carry_column,
    state_out,
    gain_out,
    finals_out,
    factor_out,
    longer,
    init,
    square,
    turned,
    states,
    factors,
    init_dot,
    taps,
    edges,
    load_sem,
):
    rows, width = chan.shape
    heads = step_raw.shape[1]
    requests = lengths.shape[0]
    inner = partial_y.shape[1]
    size = inner // heads
    state = (width - inner) // 2
    kernel = conv_inner.shape[0]
    load = pltpu.make_async_copy(init_states, init, load_sem)
    load.start()
    first_row = lax.axis_index("seq") * rows
    places = spans(lengths, deal)

    def layout(shape, dim):
        local = lax.broadcasted_iota(jnp.int32, shape, dim)
        position = local + first_row
        start = jnp.zeros(shape, jnp.int32)
        owner = jnp.zeros(shape, jnp.int32)
        for begin, _, slot in places:
            started = position >= begin
            start = jnp.where(started, begin, start)
            owner = jnp.where(started, slot, owner)
        return local, position, position - start, owner

    local_c, position_c, offset_c, owner_c = layout((rows, 1), 0)
    local_r, _, offset_r, _ = layout((1, rows), 1)
    within_c = lax.rem(local_c, BLOCK)
    within_r = lax.rem(local_r, BLOCK)
    reach_c = jnp.minimum(offset_c, within_c)
    reach_r = jnp.minimum(offset_r, within_r)
    flag_c = offset_c > within_c
    flag_r = offset_r > within_r
    reach_column[...] = reach_c

    square[...] = jnp.zeros_like(square)
    square[:, :heads] = step_raw[...]
    raw_row = square[...].T[:heads] + head_column(step_bias)
    step = jnp.maximum(raw_row, 0.0) + jnp.log1p(jnp.exp(-jnp.abs(raw_row)))
    run = -jnp.exp(head_column(decay_log)) * step
    shift = 1
    while shift < BLOCK:
        run = run + jnp.where(reach_r >= shift, pltpu.roll(run, shift, 1), 0.0)
        shift *= 2
    run_c = columns_of(run, rows)
    step_row[...] = step
    decay_row[...] = run
    decay_column[...] = run_c
    coef_c = jnp.exp(run_c)
    carry_c = jnp.where(flag_c, coef_c, 0.0)
    init_c = jnp.where(flag_c, 0.0, coef_c)
    carry_column[0:BLOCK, :] = carry_c[0:BLOCK]
    carry_column[BLOCK:, :] = carry_c[BLOCK:] * carry_c[BLOCK - 1 : BLOCK, :]

    second = lax.axis_index("col") * 2 // lax.axis_size("col") > 0
    bias = taps.at[kernel : kernel + 1]
    taps[0:kernel, :inner] = conv_inner[...]
    bias[:, :inner] = bias_inner[...]
    for back in range(kernel - 1):
        edges[back * requests : (back + 1) * requests, :inner] = edge_inner[back]
    for which in range(2):
        span = slice(inner + which * state, inner + (which + 1) * state)
        for tap in range(kernel):
            pair = conv_group[tap, which]
            taps[tap : tap + 1, span] = jnp.where(second, pair[1:2], pair[0:1])
        pair = bias_group[which]
        bias[:, span] = jnp.where(second, pair[1:2], pair[0:1])
        for back in range(kernel - 1):
            pairs = edge_group[:, back, which].astype(jnp.float32)
            edges[back * requests : (back + 1) * requests, span] = jnp.where(
                second, pairs[:, 1, :], pairs[:, 0, :]
            ).astype(jnp.bfloat16)
    longer[0:8, :] = rim[8:16, :].astype(jnp.float32)
    longer[8:, :] = chan[...].astype(jnp.float32)
    summed = bias[...] + taps[kernel - 1 : kernel, :] * longer[8:, :]
    choices = lax.broadcasted_iota(jnp.int32, (rows, edges.shape[0]), 1)
    for back in range(1, kernel):
        slot = (kernel - 1 - back + offset_c) * requests + owner_c
        lookup = ((choices == slot) & (offset_c < back)).astype(jnp.float32).astype(jnp.bfloat16)
        from_edge = jnp.dot(lookup, edges[...], preferred_element_type=jnp.float32)
        value = jnp.where(offset_c >= back, longer[8 - back : 8 - back + rows, :], from_edge)
        summed = summed + taps[kernel - 1 - back : kernel - back, :] * value
    mixed[...] = (summed * (1.0 / (1.0 + jnp.exp(-summed)))).astype(jnp.bfloat16)
    turned[...] = mixed[:, :inner].astype(jnp.float32).T.astype(jnp.bfloat16)
    states[...] = jnp.zeros_like(states)
    factors[...] = jnp.zeros_like(factors)
    init_dot[...] = jnp.zeros_like(init_dot)
    load.wait()

    def pick(values, at):
        return jnp.sum(jnp.where(local_r == at, values, jnp.zeros_like(values)), axis=1, keepdims=True)

    def emit(at, index, slot):
        reach = pick(reach_r, at)
        flagged = pick(flag_r.astype(jnp.int32), at) > 0
        run_at = pick(run, at)
        keep = (local_r <= at) & (local_r >= at - reach)
        share = jnp.exp(jnp.where(keep, run_at - run, NEVER)) * step
        share = share.astype(jnp.bfloat16).astype(jnp.float32)
        spread = (turned[...].astype(jnp.float32) * by_head(share, size)).astype(jnp.bfloat16)
        value = jnp.dot(spread, mixed[:, inner : inner + state], preferred_element_type=jnp.float32)
        coef = jnp.exp(run_at)
        carry = jnp.broadcast_to(jnp.where(flagged, coef, 0.0), (heads, state))
        start = jnp.broadcast_to(jnp.where(flagged, 0.0, coef), (heads, state))
        late = at >= BLOCK
        first_gain = jnp.broadcast_to(
            jnp.where(pick(flag_r.astype(jnp.int32), BLOCK - 1) > 0, jnp.exp(pick(run, BLOCK - 1)), 0.0),
            (heads, state),
        )
        value = value + by_head(start, size) * init[slot]
        value = value + by_head(jnp.where(late, carry, 0.0), size) * states[0]
        states[index] = value
        factors[index] = carry * jnp.where(late, first_gain, 1.0)

    def request(k, begin):
        end = begin + lengths[k]
        slot = deal[k]
        low = begin - first_row
        high = end - first_row

        @pl.when((high > 0) & (low < rows))
        def _():
            chosen = (local_c >= low) & (local_c < high) & jnp.logical_not(flag_c)
            picked = jnp.where(chosen, mixed[:, inner + state :].astype(jnp.float32), 0.0)
            init_dot[...] += lax.dot_general(
                picked.astype(jnp.bfloat16),
                init[slot].astype(jnp.bfloat16),
                (((1,), (1,)), ((), ())),
                preferred_element_type=jnp.float32,
            )

            def place(j, carry):
                at = jnp.where(j < 2, BLOCK - 1 + j * BLOCK, high - 1)
                index = jnp.where(j < 2, j, 2 + slot)

                @pl.when((at >= low) & (at < high) & (at >= 0) & (at < rows))
                def _():
                    emit(at, index, slot)

                return carry

            lax.fori_loop(0, 3, place, 0)

        return end

    lax.fori_loop(0, requests, request, jnp.int32(0))
    state_out[...] = states[1].astype(jnp.bfloat16)
    gain_out[...] = factors[1]
    finals_out[...] = states[2:].astype(jnp.bfloat16)
    factor_out[...] = factors[2:]
    carried = lax.dot_general(
        mixed[BLOCK:, inner + state :],
        states[0].astype(jnp.bfloat16),
        (((1,), (1,)), ((), ())),
        preferred_element_type=jnp.float32,
    )
    for h in range(heads):
        span = slice(h * size, (h + 1) * size)
        value = skip[h] * mixed[:, span].astype(jnp.float32)
        value = value + init_c[:, h : h + 1] * init_dot[:, span]
        partial_y[0:BLOCK, span] = value[0:BLOCK]
        partial_y[BLOCK:, span] = value[BLOCK:] + carry_c[BLOCK:, h : h + 1] * carried[:, span]


def scan(
    lengths,
    deal,
    step_bias,
    decay_log,
    skip,
    chan,
    rim,
    step_raw,
    conv_inner,
    conv_group,
    bias_inner,
    bias_group,
    edge_inner,
    edge_group,
    init_states,
):
    rows, width = chan.shape
    heads = step_raw.shape[1]
    requests, _, size, state = init_states.shape
    inner = heads * size
    smem = pl.BlockSpec(memory_space=pltpu.SMEM)
    vmem = pl.BlockSpec(memory_space=pltpu.VMEM)
    anywhere = pl.BlockSpec(memory_space=pl.ANY)
    f32, bf = jnp.float32, jnp.bfloat16
    shape = jax.ShapeDtypeStruct
    return pl.pallas_call(
        scan_kernel,
        out_shape=[
            shape((rows, inner), f32),
            shape((rows, width), bf),
            shape((rows, 128), f32),
            shape((heads, rows), f32),
            shape((heads, rows), f32),
            shape((rows, 1), jnp.int32),
            shape((rows, 128), f32),
            shape((inner, state), bf),
            shape((heads, state), f32),
            shape((requests, inner, state), bf),
            shape((requests, heads, state), f32),
        ],
        in_specs=[smem] * 5 + [vmem] * 9 + [anywhere],
        out_specs=[vmem] * 11,
        scratch_shapes=[
            pltpu.VMEM((rows + 8, width), f32),
            pltpu.VMEM((requests, inner, state), f32),
            pltpu.VMEM((rows, 128), f32),
            pltpu.VMEM((inner, rows), bf),
            pltpu.VMEM((requests + 2, inner, state), f32),
            pltpu.VMEM((requests + 2, heads, state), f32),
            pltpu.VMEM((rows, inner), f32),
            pltpu.VMEM((8, width), f32),
            pltpu.VMEM(((conv_inner.shape[0] - 1) * requests, width), bf),
            pltpu.SemaphoreType.DMA,
        ],
        compiler_params=pltpu.CompilerParams(vmem_limit_bytes=VMEM_LIMIT),
        name="scan",
    )(
        lengths,
        deal,
        step_bias,
        decay_log,
        skip,
        chan,
        rim,
        step_raw,
        conv_inner,
        conv_group,
        bias_inner[None, :],
        bias_group,
        jnp.transpose(edge_inner, (1, 0, 2)),
        edge_group,
        jnp.reshape(init_states, (requests, inner, state)),
    )


PICKS = 16
PITCH = HALF + PICKS


def slot_ends(lengths, deal, first_row, shape, dim):
    requests = lengths.shape[0]
    slots = lax.broadcasted_iota(jnp.int32, shape, dim)
    ends = jnp.zeros(shape, jnp.int32)
    end = -1 - first_row
    for k in range(requests):
        end = end + lengths[k]
        ends = jnp.where(slots == deal[k], end, ends)
    return ends


def finish_kernel(
    lengths,
    deal,
    partial_y,
    mixed,
    decay_column,
    decay_row,
    step_row,
    reach_column,
    carry_column,
    state_own,
    gain_own,
    finals_own,
    factor_own,
    gate_in,
    inner_gain,
    w_out,
    tokens,
    w_head,
    final_gain,
    hidden,
    final_states,
    logits,
    weights,
    head,
    partials,
    stage_far,
    stage_near,
    land_far,
    land_near,
    stage_far2,
    stage_near2,
    land_far2,
    land_near2,
    picks,
    rows_all,
    wide_rows,
    load_sem,
    sends,
    recvs,
    pick_sends,
    pick_recvs,
    row_sends,
    row_recvs,
    outputs,
    normed,
    scales,
    entry_held,
    land_state,
    land_gain,
    square_own,
    square_land,
    outbox,
    pair_land,
    pair_sum,
    final_land,
    far_sends,
    far_recvs,
    row_stage,
    row_land,
    early_sends,
    early_recvs,
):
    rows, feat = tokens.shape
    heads, inner = decay_row.shape[0], gate_in.shape[1]
    size = inner // heads
    state = state_own.shape[1]
    requests = lengths.shape[0]
    seq = lax.axis_size("seq")
    load_out = pltpu.make_async_copy(w_out, weights, load_sem.at[0])
    load_head = pltpu.make_async_copy(w_head, head, load_sem.at[1])
    load_out.start()
    load_head.start()
    plane = [(dr, dc) for dr in range(4) for dc in range(4) if dr or dc]
    peers = [{axis: spot(axis, shift)} for axis, shift in PLANE]
    peers += [{"seq": spot("seq", shift)} for shift in range(1, seq)]
    peers += [
        {"row": spot("row", dr), "col": spot("col", dc)}
        for dr, dc in plane
        if not ((dr == 0 and dc != 2) or (dc == 0 and dr != 2))
    ]
    greet(peers)
    extra = []

    def hand(src, dst, number, place):
        copy = pltpu.make_async_remote_copy(
            src_ref=src,
            dst_ref=dst,
            send_sem=far_sends.at[number],
            recv_sem=far_recvs.at[number],
            device_id=place,
            device_id_type=MESH,
        )
        copy.start()
        extra.append(copy)
        return copy

    hand(state_own, land_state.at[0], 0, {"seq": spot("seq", 1)})
    hand(gain_own, land_gain, 1, {"seq": spot("seq", 1)})
    hand(state_own, land_state.at[1], 2, {"seq": spot("seq", 2)})

    def inside(b, carry):
        place = pl.ds(pl.multiple_of(b * BLOCK, BLOCK), BLOCK)
        scores = lax.dot_general(
            mixed[place, inner + state :],
            mixed[place, inner : inner + state],
            (((1,), (1,)), ((), ())),
            preferred_element_type=jnp.float32,
        )
        target = lax.broadcasted_iota(jnp.int32, (BLOCK, BLOCK), 0)
        source = lax.broadcasted_iota(jnp.int32, (BLOCK, BLOCK), 1)
        keep = (source <= target) & (source >= target - reach_column[place, :])
        for h in range(heads):
            span = slice(h * size, (h + 1) * size)
            diff = decay_column[place, h : h + 1] - decay_row[h : h + 1, place]
            decay = jnp.exp(jnp.where(keep, diff, NEVER))
            weight = (scores * decay * step_row[h : h + 1, place]).astype(jnp.bfloat16)
            outputs[place, span] = partial_y[place, span] + jnp.dot(
                weight, mixed[place, span], preferred_element_type=jnp.float32
            )
        return carry

    lax.fori_loop(0, rows // BLOCK, inside, 0)
    for copy in extra:
        copy.wait_recv()
    entry = land_state[0].astype(jnp.float32) + by_head(land_gain[...], size) * land_state[
        1
    ].astype(jnp.float32)
    entry_held[...] = entry
    carried = lax.dot_general(
        mixed[:, inner + state :],
        entry.astype(jnp.bfloat16),
        (((1,), (1,)), ((), ())),
        preferred_element_type=jnp.float32,
    )
    squares = jnp.zeros((rows, 128), jnp.float32)
    left = lax.broadcasted_iota(jnp.int32, (rows, 128), 1) < size
    for tile in range(inner // 128):
        span = slice(tile * 128, (tile + 1) * 128)
        coef = jnp.where(
            left, carry_column[:, 2 * tile : 2 * tile + 1], carry_column[:, 2 * tile + 1 : 2 * tile + 2]
        )
        gate = gate_in[:, span].astype(jnp.float32)
        gated = (outputs[:, span] + coef * carried[:, span]) * (gate / (1.0 + jnp.exp(-gate)))
        squares = squares + gated * gated
        value = (gated * inner_gain[:, span]).astype(jnp.bfloat16)
        normed[0:HALF, span] = value[0:HALF]
        normed[PITCH : PITCH + HALF, span] = value[HALF:]
    square_own[...] = jnp.broadcast_to(
        jnp.sum(squares.T, axis=0, keepdims=True), square_own.shape
    )
    partner = lax.axis_index("col") + 1 - 2 * lax.rem(lax.axis_index("col"), 2)
    square_copy = hand(square_own, square_land, 3, {"col": partner})
    ends = slot_ends(lengths, deal, lax.axis_index("seq") * rows, (requests, rows), 0)
    chosen = ends == lax.broadcasted_iota(jnp.int32, (requests, rows), 1)
    chooser = chosen.astype(jnp.float32).astype(jnp.bfloat16)
    picked = jnp.dot(chooser[:, :HALF], normed[0:HALF, :], preferred_element_type=jnp.float32)
    picked = picked + jnp.dot(
        chooser[:, HALF:], normed[PITCH : PITCH + HALF, :], preferred_element_type=jnp.float32
    )
    for half in (0, 1):
        normed[half * PITCH + HALF : half * PITCH + PITCH, :] = picked.astype(jnp.bfloat16)
    load_out.wait()

    def compute(first, count, scale=None):
        def body(i, carry):
            half = lax.rem(i, 2)
            j = i // 2 + first
            dv = 2 - j // 4 - j // 8 + (j // 12) * 2
            du = 2 - lax.rem(j, 4) - lax.rem(j, 4) // 2 + (lax.rem(j, 4) // 3) * 2
            block = block_of(half, du, dv)
            place = pl.ds(pl.multiple_of(half * PITCH, PICKS), PITCH)
            value = jnp.dot(
                normed[place, :],
                weights[:, pl.ds(pl.multiple_of(block * feat, feat), feat)],
                preferred_element_type=jnp.float32,
            )
            if scale is not None:
                value = value * scale[place, :]
            partials[half, j] = value
            return carry

        lax.fori_loop(0, 2 * count, body, 0)

    started = {}

    def send(half, number, src, dst, axis, shift):
        copy = remote(src, dst, sends.at[half], recvs.at[half], number, axis, shift)
        copy.start()
        started[half, number] = copy

    def far(half, values, stage, land, number, axis):
        for side in (0, 1):
            stage[side] = values[side * 128 : side * 128 + 128].astype(jnp.bfloat16)
            send(half, number + side, stage.at[side], land.at[side], axis, 1 - 2 * side)

    def near(half, side, values, far_land, far_number, stage, land, number, axis):
        started[half, far_number + side].wait_recv()
        extra = far_land[side].astype(jnp.float32)
        keep = slice(128 - 128 * side, 256 - 128 * side)
        mix = slice(128 * side, 128 * side + 128)
        stage[side, mix] = (values[mix] + extra).astype(jnp.bfloat16)
        stage[side, keep] = values[keep].astype(jnp.bfloat16)
        send(half, number + side, stage.at[side], land.at[side], axis, 1 - 2 * side)

    compute(0, 4)
    square_copy.wait_recv()
    both = square_own[0:1, :] + square_land[0:1, :]
    scale_row = lax.rsqrt(both / (2 * inner) + EPSILON)
    scale_tile = jnp.broadcast_to(scale_row, (128, rows)).T
    wide_scale = jnp.concatenate([scale_tile, scale_tile], axis=1)
    pick_scale = jnp.broadcast_to(
        jnp.sum(jnp.where(chosen, scale_row, 0.0), axis=1, keepdims=True), (requests, feat)
    )
    for half in (0, 1):
        start = half * PITCH
        scales[start : start + HALF, :] = wide_scale[half * HALF : half * HALF + HALF]
        scales[start + HALF : start + PITCH, :] = pick_scale
    for k in range(4):
        for half in (0, 1):
            far(
                half,
                partials[half, k, 0:HALF] * scales[half * PITCH : half * PITCH + HALF, :],
                stage_far.at[half, k],
                land_far.at[half, k],
                2 * k,
                AXES[half][1],
            )
    compute(4, 12, scales)
    row_copies = []
    for j in range(15):
        dv, du = (2, 1, -1, 0)[j // 4], (2, 1, -1, 0)[j % 4]
        value = partials[0, j, HALF:PITCH]
        if j < 4:
            value = value * pick_scale
        row_stage[j] = value.astype(jnp.bfloat16)
        copy = pltpu.make_async_remote_copy(
            src_ref=row_stage.at[j],
            dst_ref=row_land.at[j],
            send_sem=early_sends.at[j],
            recv_sem=early_recvs.at[j],
            device_id={"row": spot("row", dv), "col": spot("col", du)},
            device_id_type=MESH,
        )
        copy.start()
        row_copies.append(copy)
    core = lax.rem(lax.axis_index("seq"), 2)
    chip = lax.axis_index("seq") // 2
    chips = seq // 2

    def fill(o, carry):
        value = finals_own[o].astype(jnp.float32) + by_head(factor_own[o], size) * entry_held[...]
        outbox[lax.rem(o // 2, 2), o // 4, lax.rem(o, 2)] = value.astype(jnp.bfloat16)
        return carry

    lax.fori_loop(0, requests, fill, 0)
    pair_copy = hand(outbox.at[1 - core], pair_land, 4, {"seq": spot("seq", 1 - 2 * core)})
    for k in range(4):
        for half in (0, 1):
            for side in (0, 1):
                near(
                    half,
                    side,
                    partials[half, 4 + 4 * side + k, 0:HALF],
                    land_far.at[half, k],
                    2 * k,
                    stage_near.at[half, k],
                    land_near.at[half, k],
                    8 + 2 * k,
                    AXES[half][1],
                )
    row_total = partials[0, 15, HALF:PITCH]
    row_total = row_total + jnp.dot(chooser, tokens[...], preferred_element_type=jnp.float32)
    for j, copy in enumerate(row_copies):
        copy.wait_recv()
        row_total = row_total + row_land[j].astype(jnp.float32)
    picks[0] = row_total.astype(jnp.bfloat16)
    handed = []
    for shift in range(1, seq):
        copy = remote(
            picks.at[0], picks.at[shift], pick_sends, pick_recvs, shift, "seq", shift
        )
        copy.start()
        handed.append(copy)
    own = block_of(0, 0, 0)

    def gather_rows():
        for copy in handed[: seq - 1]:
            copy.wait_recv()
        whole = picks[0].astype(jnp.float32)
        for shift in range(1, seq):
            whole = whole + picks[shift].astype(jnp.float32)
        rows_all[own] = whole.astype(jnp.bfloat16)
        for number, (dr, dc) in enumerate(plane):
            copy = pltpu.make_async_remote_copy(
                src_ref=rows_all.at[own],
                dst_ref=rows_all.at[own],
                send_sem=row_sends.at[number],
                recv_sem=row_recvs.at[number],
                device_id={"row": spot("row", dr), "col": spot("col", dc)},
                device_id_type=MESH,
            )
            copy.start()
            handed.append(copy)

    pair_copy.wait_recv()
    for d in range(chips):
        there = lax.rem(chip + d, chips)
        pair_sum[d] = (
            outbox[core, there].astype(jnp.float32) + pair_land[there].astype(jnp.float32)
        ).astype(jnp.bfloat16)
    final_copies = [
        hand(pair_sum.at[d], final_land.at[d - 1], 4 + d, {"seq": spot("seq", 2 * d)})
        for d in range(1, chips)
    ]
    for k in range(4):
        if k == 2:
            gather_rows()
        for half in (0, 1):
            axis = AXES[half][0]
            total = partials[half, 12 + k, 0:HALF]
            for side in (0, 1):
                started[half, 8 + 2 * k + side].wait_recv()
                total = total + land_near[half, k, side].astype(jnp.float32)
            if k == 0:
                far(half, total, stage_far2.at[half], land_far2.at[half], 16, axis)
            elif k < 3:
                near(
                    half,
                    k - 1,
                    total,
                    land_far2.at[half],
                    16,
                    stage_near2.at[half],
                    land_near2.at[half],
                    18,
                    axis,
                )
            else:
                for side in (0, 1):
                    started[half, 18 + side].wait_recv()
                    total = total + land_near2[half, side].astype(jnp.float32)
                place = slice(half * HALF, half * HALF + HALF)
                hidden[place, :] = (tokens[place, :].astype(jnp.float32) + total).astype(
                    jnp.bfloat16
                )
    for copy in handed[seq - 1 :]:
        copy.wait_recv()
    for copy in final_copies:
        copy.wait_recv()
    final = pair_sum[0].astype(jnp.float32)
    for d in range(1, chips):
        final = final + final_land[d - 1].astype(jnp.float32)
    final_states[...] = final
    load_head.wait()
    total = jnp.zeros((requests, 128), jnp.float32)
    for block in range(len(plane) + 1):
        value = rows_all[block].astype(jnp.float32)
        wide_rows[:, block * feat : (block + 1) * feat] = value
        total = total + value[:, :128] * value[:, :128] + value[:, 128:] * value[:, 128:]
    depth = w_head.shape[0]
    scale = lax.rsqrt(jnp.sum(total, axis=1, keepdims=True) / depth + EPSILON)
    head_in = (wide_rows[...] * scale * final_gain[...]).astype(jnp.bfloat16)
    logits[...] = jnp.dot(head_in, head[...], preferred_element_type=jnp.float32)
    for copy in handed:
        copy.wait_send()
    for copy in list(started.values()) + extra + row_copies:
        copy.wait_send()


def finish(lengths, deal, arrays, gate_in, inner_gain, w_out, tokens, w_head, final_gain):
    rows, feat = tokens.shape
    inner, depth = w_out.shape
    requests = lengths.shape[0]
    vocab = w_head.shape[1]
    seq = lax.axis_size("seq")
    state = arrays[7].shape[1]
    heads = arrays[8].shape[0]
    slots = requests // seq
    smem = pl.BlockSpec(memory_space=pltpu.SMEM)
    vmem = pl.BlockSpec(memory_space=pltpu.VMEM)
    anywhere = pl.BlockSpec(memory_space=pl.ANY)
    bf, f32 = jnp.bfloat16, jnp.float32
    return pl.pallas_call(
        finish_kernel,
        out_shape=[
            jax.ShapeDtypeStruct((rows, feat), bf),
            jax.ShapeDtypeStruct((slots, inner, state), f32),
            jax.ShapeDtypeStruct((requests, vocab), f32),
        ],
        in_specs=[smem, smem] + [vmem] * 13 + [anywhere, vmem, anywhere, vmem],
        out_specs=[vmem] * 3,
        scratch_shapes=[
            pltpu.VMEM((inner, depth), bf),
            pltpu.VMEM((depth, vocab), bf),
            pltpu.VMEM((2, 16, PITCH, feat), f32),
            pltpu.VMEM((2, 4, 2, 128, feat), bf),
            pltpu.VMEM((2, 4, 2, 256, feat), bf),
            pltpu.VMEM((2, 4, 2, 128, feat), bf),
            pltpu.VMEM((2, 4, 2, 256, feat), bf),
            pltpu.VMEM((2, 2, 128, feat), bf),
            pltpu.VMEM((2, 2, 256, feat), bf),
            pltpu.VMEM((2, 2, 128, feat), bf),
            pltpu.VMEM((2, 2, 256, feat), bf),
            pltpu.VMEM((seq, requests, feat), bf),
            pltpu.VMEM((16, requests, feat), bf),
            pltpu.VMEM((requests, depth), f32),
            pltpu.SemaphoreType.DMA((2,)),
            pltpu.SemaphoreType.DMA((2, 20)),
            pltpu.SemaphoreType.DMA((2, 20)),
            pltpu.SemaphoreType.DMA((seq,)),
            pltpu.SemaphoreType.DMA((seq,)),
            pltpu.SemaphoreType.DMA((15,)),
            pltpu.SemaphoreType.DMA((15,)),
            pltpu.VMEM((rows, inner), f32),
            pltpu.VMEM((2 * PITCH, inner), bf),
            pltpu.VMEM((2 * PITCH, feat), f32),
            pltpu.VMEM((inner, state), f32),
            pltpu.VMEM((2, inner, state), bf),
            pltpu.VMEM((heads, state), f32),
            pltpu.VMEM((8, rows), f32),
            pltpu.VMEM((8, rows), f32),
            pltpu.VMEM((2, seq // 2, slots, inner, state), bf),
            pltpu.VMEM((seq // 2, slots, inner, state), bf),
            pltpu.VMEM((seq // 2, slots, inner, state), bf),
            pltpu.VMEM((seq // 2 - 1, slots, inner, state), bf),
            pltpu.SemaphoreType.DMA((8,)),
            pltpu.SemaphoreType.DMA((8,)),
            pltpu.VMEM((15, requests, feat), bf),
            pltpu.VMEM((15, requests, feat), bf),
            pltpu.SemaphoreType.DMA((15,)),
            pltpu.SemaphoreType.DMA((15,)),
        ],
        compiler_params=pltpu.CompilerParams(
            collective_id=1, has_side_effects=True, vmem_limit_bytes=VMEM_LIMIT
        ),
        name="finish",
    )(
        lengths,
        deal,
        *arrays,
        gate_in,
        inner_gain[None, :],
        w_out,
        tokens,
        w_head,
        final_gain[None, :],
    )


def deliver_kernel(*refs):
    count = len(refs) // 2
    sems = refs[-1]
    copies = [
        pltpu.make_async_copy(refs[i], refs[count + i], sems.at[i]) for i in range(count)
    ]
    for copy in copies:
        copy.start()
    for copy in copies:
        copy.wait()


def deliver(*arrays):
    return pl.pallas_call(
        deliver_kernel,
        out_shape=[jax.ShapeDtypeStruct(a.shape, a.dtype) for a in arrays],
        in_specs=[pl.BlockSpec(memory_space=pltpu.VMEM)] * len(arrays),
        out_specs=[pl.BlockSpec(memory_space=pl.ANY)] * len(arrays),
        scratch_shapes=[pltpu.SemaphoreType.DMA((len(arrays),))],
        name="deliver",
    )(*arrays)


def per_device(
    tokens,
    lengths,
    deal,
    pre_gain,
    w_inner,
    w_group,
    w_step,
    conv_inner,
    conv_group,
    conv_bias_inner,
    conv_bias_group,
    edge_inner,
    edge_group,
    init_states,
    step_bias,
    decay_log,
    skip,
    inner_gain,
    w_out,
    final_gain,
    w_head,
):
    inner = conv_inner.shape[1]
    state = w_group.shape[3]
    heads = w_step.shape[1]
    gate_in, chan, step_raw, rim = project(tokens, w_inner, w_group, w_step, pre_gain)
    arrays = scan(
        lengths,
        deal,
        step_bias,
        decay_log,
        skip,
        chan,
        rim,
        step_raw,
        conv_inner,
        conv_group,
        conv_bias_inner,
        conv_bias_group,
        edge_inner,
        edge_group,
        init_states,
    )
    hidden_out, final_states, logits = finish(
        lengths, deal, arrays, gate_in, inner_gain, w_out, tokens, w_head, final_gain
    )
    hidden_out, final_states, logits = deliver(hidden_out, final_states, logits)
    final_states = jnp.reshape(
        final_states, (final_states.shape[0], heads, inner // heads, state)
    )
    return (hidden_out, final_states, logits)


def solution(mesh):
    in_specs = (
        P("seq", ("row", "col")),
        P(),
        P(),
        P(),
        P(None, None, ("row", "col")),
        P(None, None, "row", None),
        P(None, ("row", "col")),
        P(None, ("row", "col")),
        P(None, None, "row", None),
        P(("row", "col")),
        P(None, "row", None),
        P(None, None, ("row", "col")),
        P(None, None, None, "row", None),
        P(None, ("row", "col"), None, None),
        P(("row", "col")),
        P(("row", "col")),
        P(("row", "col")),
        P(("row", "col")),
        P(("row", "col"), None),
        P(),
        P(None, ("seq", "row", "col")),
    )
    out_specs = (
        P("seq", ("row", "col")),
        P("seq", ("row", "col"), None, None),
        P(None, ("seq", "row", "col")),
    )
    return jax.shard_map(
        per_device, mesh=mesh, in_specs=in_specs, out_specs=out_specs, check_vma=False
    )
```

```python
import jax
import jax.numpy as jnp
from jax import lax
from jax.experimental import pallas as pl
from jax.experimental.pallas import tpu as pltpu
from jax.sharding import PartitionSpec as P

BLOCK = 256


EPSILON = 1e-05


MESH = pl.DeviceIdType.MESH
HALF = 256
FEAT = 256
VMEM_LIMIT = 62 * 1024 * 1024


def spot(axis, shift):
    size = lax.axis_size(axis)
    return lax.rem(lax.axis_index(axis) + shift + size, size)


def block_of(half, du, dv):
    row = spot("row", dv + half * (du - dv))
    col = spot("col", du + half * (dv - du))
    return row * lax.axis_size("col") + col


def remote(src, dst, sends, recvs, place, axis, shift):
    return pltpu.make_async_remote_copy(
        src_ref=src,
        dst_ref=dst,
        send_sem=sends.at[place],
        recv_sem=recvs.at[place],
        device_id={axis: spot(axis, shift)},
        device_id_type=MESH,
    )


def greet(peers):
    barrier = pltpu.get_barrier_semaphore()
    for peer in peers:
        pl.semaphore_signal(barrier, inc=1, device_id=peer, device_id_type=MESH)
    pl.semaphore_wait(barrier, len(peers))


PLANE = (("row", 1), ("row", -1), ("col", 1), ("col", -1))
AXES = (("col", "row"), ("row", "col"))
ORDER = (0, -1, 1, 2)
CHUNK = 64
PARTS = 4


def project_kernel(
    tokens,
    w_inner,
    w_group,
    w_step,
    gain,
    gate_out,
    chan_out,
    step_out,
    rim_out,
    raw_inner,
    raw_group,
    weights,
    wide_inner,
    wide_group,
    held,
    total,
    total_step,
    squares,
    load_sem,
    own_sem,
    sends,
    recvs,
    rim_stage,
    rim_land,
    rim_sems,
):
    depth = weights.shape[0]
    width = gate_out.shape[1]
    lanes = 128
    rows_part = depth // PARTS
    flat_inner = w_inner.reshape(2 * depth, width)
    flat_group = w_group.reshape(4 * depth, lanes)
    loads = []
    for part in range(PARTS):
        loads.append(
            (
                pltpu.make_async_copy(
                    flat_inner.at[pl.ds(2 * rows_part * part, 2 * rows_part)],
                    raw_inner.at[pl.ds(2 * rows_part * part, 2 * rows_part)],
                    load_sem.at[0, part],
                ),
                pltpu.make_async_copy(
                    flat_group.at[pl.ds(4 * rows_part * part, 4 * rows_part)],
                    raw_group.at[pl.ds(4 * rows_part * part, 4 * rows_part)],
                    load_sem.at[1, part],
                ),
            )
        )
    for part in range(PARTS):
        loads[part][0].start()
        loads[part][1].start()
    own = block_of(0, 0, 0)
    own_copy = pltpu.make_async_copy(tokens, held.at[own], own_sem)
    own_copy.start()
    greet([{axis: spot(axis, shift)} for axis, shift in PLANE + (("seq", 1), ("seq", -1))])
    messages = {}

    def send(half, number, du, dv, axis, shift, first, count, from_own=False):
        block = block_of(half, du, dv)
        rows = pl.ds(half * HALF + first, count)
        src = tokens.at[rows] if from_own else held.at[block, rows]
        copy = remote(
            src, held.at[block, rows], sends.at[half], recvs.at[half], number, axis, shift
        )
        copy.start()
        messages[half, number] = copy

    def arrive(half, *numbers):
        for number in numbers:
            messages[half, number].wait_recv()

    def spread(half, k, from_own=False):
        axis = AXES[half][1]
        send(half, 4 + 4 * k, ORDER[k], 0, axis, 1, 0, HALF, from_own)
        send(half, 5 + 4 * k, ORDER[k], 0, axis, -1, 0, HALF, from_own)

    def relay(half, k):
        axis = AXES[half][1]
        arrive(half, 4 + 4 * k)
        send(half, 6 + 4 * k, ORDER[k], -1, axis, 1, 0, HALF // 2)
        arrive(half, 5 + 4 * k)
        send(half, 7 + 4 * k, ORDER[k], 1, axis, -1, HALF // 2, HALF // 2)

    for half in (0, 1):
        axis = AXES[half][0]
        send(half, 0, 0, 0, axis, 1, 0, HALF, True)
        send(half, 1, 0, 0, axis, -1, 0, HALF, True)
    for half in (0, 1):
        spread(half, 0, True)
    group_local = lax.axis_index("col") * 2 // lax.axis_size("col")

    def untangle(part):
        loads[part][0].wait()
        loads[part][1].wait()

        def body(i, carry):
            base = pl.multiple_of(part * rows_part + i * CHUNK, CHUNK)
            for j in range(width // lanes):
                wide_inner[j] = raw_inner[
                    pl.ds(2 * base, 2 * CHUNK), j * lanes : (j + 1) * lanes
                ].astype(jnp.float32)
            wide_group[...] = raw_group[pl.ds(4 * base, 4 * CHUNK), :].astype(jnp.float32)
            for which in range(2):
                for j in range(width // lanes):
                    weights[
                        pl.ds(base, CHUNK), which * width + j * lanes : which * width + (j + 1) * lanes
                    ] = wide_inner[j, pl.ds(which, CHUNK, stride=2), :].astype(jnp.bfloat16)
                start = 2 * width + which * lanes
                weights[pl.ds(base, CHUNK), start : start + lanes] = wide_group[
                    pl.ds(2 * which + group_local, CHUNK, stride=4), :
                ].astype(jnp.bfloat16)
            return carry

        lax.fori_loop(0, rows_part // CHUNK, body, 0)

    total[...] = jnp.zeros_like(total)
    total_step[...] = jnp.zeros_like(total_step)
    squares[...] = jnp.zeros_like(squares)

    def multiply(half, places):
        rows = pl.ds(pl.multiple_of(half * HALF, HALF), HALF)
        value = 0.0
        step_value = 0.0
        square = 0.0
        for du, dv in places:
            block = block_of(half, du, dv)
            column = pl.multiple_of(block * FEAT, FEAT)
            wide = held[block, rows, :].astype(jnp.float32)
            square = square + wide[:, :lanes] * wide[:, :lanes]
            square = square + wide[:, lanes:] * wide[:, lanes:]
            scaled = (wide * gain[:, pl.ds(column, FEAT)]).astype(jnp.bfloat16)
            value = value + jnp.dot(
                scaled, weights[pl.ds(column, FEAT), :], preferred_element_type=jnp.float32
            )
            step_value = step_value + lax.dot_general(
                scaled,
                w_step[:, pl.ds(column, FEAT)],
                (((1,), (1,)), ((), ())),
                preferred_element_type=jnp.float32,
            )
        squares[rows, :] += square
        total[rows, :] += value
        total_step[rows, :] += step_value

    def run(count, pick):
        def body(i, carry):
            multiply(lax.rem(i, 2), pick(i // 2))
            return carry

        lax.fori_loop(0, 2 * count, body, 0)

    untangle(0)
    for half in (0, 1):
        arrive(half, 0)
        send(half, 2, -1, 0, AXES[half][0], 1, 0, HALF // 2)
        spread(half, 1)
        arrive(half, 1)
        send(half, 3, 1, 0, AXES[half][0], -1, HALF // 2, HALF // 2)
        spread(half, 2)
    untangle(1)
    for half in (0, 1):
        relay(half, 0)
    untangle(2)
    for half in (0, 1):
        arrive(half, 2, 3)
        spread(half, 3)
    untangle(3)
    own_copy.wait()
    run(1, lambda j: ((0, 0), (1, 0)))
    for half in (0, 1):
        relay(half, 1)
    run(1, lambda j: ((2, 0), (-1, 0)))
    for half in (0, 1):
        relay(half, 2)
    run(1, lambda j: ((0, -1), (0, 1), (-1, -1), (-1, 1)))
    for half in (0, 1):
        relay(half, 3)
    run(1, lambda j: ((1, -1), (1, 1), (2, -1), (2, 1)))
    for k in (0, 2):
        for half in (0, 1):
            arrive(half, 6 + 4 * k, 7 + 4 * k, 10 + 4 * k, 11 + 4 * k)
        run(1, lambda j: ((ORDER[k], 2), (ORDER[k + 1], 2)))
    for half in (0, 1):
        for number in range(20):
            messages[half, number].wait_send()
    inv_rms = lax.rsqrt(jnp.sum(squares[...], axis=1, keepdims=True) / depth + EPSILON)
    last = total.shape[0] - rim_stage.shape[0]
    rim_stage[...] = (total[last:, width:] * inv_rms[last:]).astype(jnp.bfloat16)
    rim_copy = pltpu.make_async_remote_copy(
        src_ref=rim_stage,
        dst_ref=rim_land,
        send_sem=rim_sems.at[0],
        recv_sem=rim_sems.at[1],
        device_id={"seq": spot("seq", 1)},
        device_id_type=MESH,
    )
    rim_copy.start()
    gate_out[...] = (total[:, :width] * inv_rms).astype(jnp.bfloat16)
    chan_out[...] = (total[:, width:] * inv_rms).astype(jnp.bfloat16)
    step_out[...] = total_step[...] * inv_rms
    rim_copy.wait()
    rim_out[...] = rim_land[...]


def project(tokens, w_inner, w_group, w_step, pre_gain):
    rows, feat = tokens.shape
    depth, _, width = w_inner.shape
    heads = w_step.shape[1]
    state = w_group.shape[3]
    blocks = depth // feat
    columns = 2 * width + 2 * state
    vmem = pl.BlockSpec(memory_space=pltpu.VMEM)
    anywhere = pl.BlockSpec(memory_space=pl.ANY)
    return pl.pallas_call(
        project_kernel,
        out_shape=[
            jax.ShapeDtypeStruct((rows, width), jnp.bfloat16),
            jax.ShapeDtypeStruct((rows, width + 2 * state), jnp.bfloat16),
            jax.ShapeDtypeStruct((rows, heads), jnp.float32),
            jax.ShapeDtypeStruct((16, width + 2 * state), jnp.bfloat16),
        ],
        in_specs=[anywhere, anywhere, anywhere, vmem, vmem],
        out_specs=[vmem] * 4,
        scratch_shapes=[
            pltpu.VMEM((2 * depth, width), jnp.bfloat16),
            pltpu.VMEM((4 * depth, state), jnp.bfloat16),
            pltpu.VMEM((depth, columns), jnp.bfloat16),
            pltpu.VMEM((width // 128, 2 * CHUNK, 128), jnp.float32),
            pltpu.VMEM((4 * CHUNK, 128), jnp.float32),
            pltpu.VMEM((blocks, rows, feat), jnp.bfloat16),
            pltpu.VMEM((rows, columns), jnp.float32),
            pltpu.VMEM((rows, heads), jnp.float32),
            pltpu.VMEM((rows, 128), jnp.float32),
            pltpu.SemaphoreType.DMA((2, PARTS)),
            pltpu.SemaphoreType.DMA,
            pltpu.SemaphoreType.DMA((2, 20)),
            pltpu.SemaphoreType.DMA((2, 20)),
            pltpu.VMEM((16, width + 2 * state), jnp.bfloat16),
            pltpu.VMEM((16, width + 2 * state), jnp.bfloat16),
            pltpu.SemaphoreType.DMA((2,)),
        ],
        compiler_params=pltpu.CompilerParams(
            collective_id=0, has_side_effects=True, vmem_limit_bytes=VMEM_LIMIT
        ),
        name="project",
    )(tokens, w_inner, w_group, w_step.T, pre_gain[None, :])


NEVER = -1e30


def spans(lengths, deal):
    found = []
    begin = 0
    for k in range(lengths.shape[0]):
        end = begin + lengths[k]
        found.append((begin, end, deal[k]))
        begin = end
    return found


def head_column(values):
    heads = values.shape[0]
    places = lax.broadcasted_iota(jnp.int32, (heads, 1), 0)
    column = jnp.zeros((heads, 1), jnp.float32)
    for h in range(heads):
        column = jnp.where(places == h, values[h], column)
    return column


def by_head(tile, size):
    heads, width = tile.shape
    return jnp.reshape(
        jnp.broadcast_to(tile[:, None, :], (heads, size, width)), (heads * size, width)
    )


def columns_of(rows_by_head, count):
    heads = rows_by_head.shape[0]
    padding = jnp.zeros((128 - heads, count), jnp.float32)
    return jnp.concatenate([rows_by_head, padding], axis=0).T


def scan_kernel(
    lengths,
    deal,
    step_bias,
    decay_log,
    skip,
    chan,
    rim,
    step_raw,
    conv_inner,
    conv_group,
    bias_inner,
    bias_group,
    edge_inner,
    edge_group,
    init_states,
    partial_y,
    mixed,
    decay_column,
    decay_row,
    step_row,
    reach_column,
    carry_column,
    state_out,
    gain_out,
    finals_out,
    factor_out,
    longer,
    init,
    square,
    turned,
    states,
    factors,
    init_dot,
    taps,
    edges,
    load_sem,
):
    rows, width = chan.shape
    heads = step_raw.shape[1]
    requests = lengths.shape[0]
    inner = partial_y.shape[1]
    size = inner // heads
    state = (width - inner) // 2
    kernel = conv_inner.shape[0]
    load = pltpu.make_async_copy(init_states, init, load_sem)
    load.start()
    first_row = lax.axis_index("seq") * rows
    places = spans(lengths, deal)

    def layout(shape, dim):
        local = lax.broadcasted_iota(jnp.int32, shape, dim)
        position = local + first_row
        start = jnp.zeros(shape, jnp.int32)
        owner = jnp.zeros(shape, jnp.int32)
        for begin, _, slot in places:
            started = position >= begin
            start = jnp.where(started, begin, start)
            owner = jnp.where(started, slot, owner)
        return local, position, position - start, owner

    local_c, position_c, offset_c, owner_c = layout((rows, 1), 0)
    local_r, _, offset_r, _ = layout((1, rows), 1)
    within_c = lax.rem(local_c, BLOCK)
    within_r = lax.rem(local_r, BLOCK)
    reach_c = jnp.minimum(offset_c, within_c)
    reach_r = jnp.minimum(offset_r, within_r)
    flag_c = offset_c > within_c
    flag_r = offset_r > within_r
    reach_column[...] = reach_c

    square[...] = jnp.zeros_like(square)
    square[:, :heads] = step_raw[...]
    raw_row = square[...].T[:heads] + head_column(step_bias)
    step = jnp.maximum(raw_row, 0.0) + jnp.log1p(jnp.exp(-jnp.abs(raw_row)))
    run = -jnp.exp(head_column(decay_log)) * step
    shift = 1
    while shift < BLOCK:
        run = run + jnp.where(reach_r >= shift, pltpu.roll(run, shift, 1), 0.0)
        shift *= 2
    run_c = columns_of(run, rows)
    step_row[...] = step
    decay_row[...] = run
    decay_column[...] = run_c
    coef_c = jnp.exp(run_c)
    carry_c = jnp.where(flag_c, coef_c, 0.0)
    init_c = jnp.where(flag_c, 0.0, coef_c)
    carry_column[0:BLOCK, :] = carry_c[0:BLOCK]
    carry_column[BLOCK:, :] = carry_c[BLOCK:] * carry_c[BLOCK - 1 : BLOCK, :]

    second = lax.axis_index("col") * 2 // lax.axis_size("col") > 0
    bias = taps.at[kernel : kernel + 1]
    taps[0:kernel, :inner] = conv_inner[...]
    bias[:, :inner] = bias_inner[...]
    for back in range(kernel - 1):
        edges[back * requests : (back + 1) * requests, :inner] = edge_inner[back]
    for which in range(2):
        span = slice(inner + which * state, inner + (which + 1) * state)
        for tap in range(kernel):
            pair = conv_group[tap, which]
            taps[tap : tap + 1, span] = jnp.where(second, pair[1:2], pair[0:1])
        pair = bias_group[which]
        bias[:, span] = jnp.where(second, pair[1:2], pair[0:1])
        for back in range(kernel - 1):
            pairs = edge_group[:, back, which].astype(jnp.float32)
            edges[back * requests : (back + 1) * requests, span] = jnp.where(
                second, pairs[:, 1, :], pairs[:, 0, :]
            ).astype(jnp.bfloat16)
    longer[0:8, :] = rim[8:16, :].astype(jnp.float32)
    longer[8:, :] = chan[...].astype(jnp.float32)
    summed = bias[...] + taps[kernel - 1 : kernel, :] * longer[8:, :]
    choices = lax.broadcasted_iota(jnp.int32, (rows, edges.shape[0]), 1)
    for back in range(1, kernel):
        slot = (kernel - 1 - back + offset_c) * requests + owner_c
        lookup = ((choices == slot) & (offset_c < back)).astype(jnp.float32).astype(jnp.bfloat16)
        from_edge = jnp.dot(lookup, edges[...], preferred_element_type=jnp.float32)
        value = jnp.where(offset_c >= back, longer[8 - back : 8 - back + rows, :], from_edge)
        summed = summed + taps[kernel - 1 - back : kernel - back, :] * value
    mixed[...] = (summed * (1.0 / (1.0 + jnp.exp(-summed)))).astype(jnp.bfloat16)
    turned[...] = mixed[:, :inner].astype(jnp.float32).T.astype(jnp.bfloat16)
    states[...] = jnp.zeros_like(states)
    factors[...] = jnp.zeros_like(factors)
    init_dot[...] = jnp.zeros_like(init_dot)
    load.wait()

    def pick(values, at):
        return jnp.sum(jnp.where(local_r == at, values, jnp.zeros_like(values)), axis=1, keepdims=True)

    def emit(at, index, slot):
        reach = pick(reach_r, at)
        flagged = pick(flag_r.astype(jnp.int32), at) > 0
        run_at = pick(run, at)
        keep = (local_r <= at) & (local_r >= at - reach)
        share = jnp.exp(jnp.where(keep, run_at - run, NEVER)) * step
        share = share.astype(jnp.bfloat16).astype(jnp.float32)
        spread = (turned[...].astype(jnp.float32) * by_head(share, size)).astype(jnp.bfloat16)
        value = jnp.dot(spread, mixed[:, inner : inner + state], preferred_element_type=jnp.float32)
        coef = jnp.exp(run_at)
        carry = jnp.broadcast_to(jnp.where(flagged, coef, 0.0), (heads, state))
        start = jnp.broadcast_to(jnp.where(flagged, 0.0, coef), (heads, state))
        late = at >= BLOCK
        first_gain = jnp.broadcast_to(
            jnp.where(pick(flag_r.astype(jnp.int32), BLOCK - 1) > 0, jnp.exp(pick(run, BLOCK - 1)), 0.0),
            (heads, state),
        )
        value = value + by_head(start, size) * init[slot]
        value = value + by_head(jnp.where(late, carry, 0.0), size) * states[0]
        states[index] = value
        factors[index] = carry * jnp.where(late, first_gain, 1.0)

    def request(k, begin):
        end = begin + lengths[k]
        slot = deal[k]
        low = begin - first_row
        high = end - first_row

        @pl.when((high > 0) & (low < rows))
        def _():
            chosen = (local_c >= low) & (local_c < high) & jnp.logical_not(flag_c)
            picked = jnp.where(chosen, mixed[:, inner + state :].astype(jnp.float32), 0.0)
            init_dot[...] += lax.dot_general(
                picked.astype(jnp.bfloat16),
                init[slot].astype(jnp.bfloat16),
                (((1,), (1,)), ((), ())),
                preferred_element_type=jnp.float32,
            )

            def place(j, carry):
                at = jnp.where(j < 2, BLOCK - 1 + j * BLOCK, high - 1)
                index = jnp.where(j < 2, j, 2 + slot)

                @pl.when((at >= low) & (at < high) & (at >= 0) & (at < rows))
                def _():
                    emit(at, index, slot)

                return carry

            lax.fori_loop(0, 3, place, 0)

        return end

    lax.fori_loop(0, requests, request, jnp.int32(0))
    state_out[...] = states[1].astype(jnp.bfloat16)
    gain_out[...] = factors[1]
    finals_out[...] = states[2:].astype(jnp.bfloat16)
    factor_out[...] = factors[2:]
    carried = lax.dot_general(
        mixed[BLOCK:, inner + state :],
        states[0].astype(jnp.bfloat16),
        (((1,), (1,)), ((), ())),
        preferred_element_type=jnp.float32,
    )
    for h in range(heads):
        span = slice(h * size, (h + 1) * size)
        value = skip[h] * mixed[:, span].astype(jnp.float32)
        value = value + init_c[:, h : h + 1] * init_dot[:, span]
        partial_y[0:BLOCK, span] = value[0:BLOCK]
        partial_y[BLOCK:, span] = value[BLOCK:] + carry_c[BLOCK:, h : h + 1] * carried[:, span]


def scan(
    lengths,
    deal,
    step_bias,
    decay_log,
    skip,
    chan,
    rim,
    step_raw,
    conv_inner,
    conv_group,
    bias_inner,
    bias_group,
    edge_inner,
    edge_group,
    init_states,
):
    rows, width = chan.shape
    heads = step_raw.shape[1]
    requests, _, size, state = init_states.shape
    inner = heads * size
    smem = pl.BlockSpec(memory_space=pltpu.SMEM)
    vmem = pl.BlockSpec(memory_space=pltpu.VMEM)
    anywhere = pl.BlockSpec(memory_space=pl.ANY)
    f32, bf = jnp.float32, jnp.bfloat16
    shape = jax.ShapeDtypeStruct
    return pl.pallas_call(
        scan_kernel,
        out_shape=[
            shape((rows, inner), f32),
            shape((rows, width), bf),
            shape((rows, 128), f32),
            shape((heads, rows), f32),
            shape((heads, rows), f32),
            shape((rows, 1), jnp.int32),
            shape((rows, 128), f32),
            shape((inner, state), bf),
            shape((heads, state), f32),
            shape((requests, inner, state), bf),
            shape((requests, heads, state), f32),
        ],
        in_specs=[smem] * 5 + [vmem] * 9 + [anywhere],
        out_specs=[vmem] * 11,
        scratch_shapes=[
            pltpu.VMEM((rows + 8, width), f32),
            pltpu.VMEM((requests, inner, state), f32),
            pltpu.VMEM((rows, 128), f32),
            pltpu.VMEM((inner, rows), bf),
            pltpu.VMEM((requests + 2, inner, state), f32),
            pltpu.VMEM((requests + 2, heads, state), f32),
            pltpu.VMEM((rows, inner), f32),
            pltpu.VMEM((8, width), f32),
            pltpu.VMEM(((conv_inner.shape[0] - 1) * requests, width), bf),
            pltpu.SemaphoreType.DMA,
        ],
        compiler_params=pltpu.CompilerParams(vmem_limit_bytes=VMEM_LIMIT),
        name="scan",
    )(
        lengths,
        deal,
        step_bias,
        decay_log,
        skip,
        chan,
        rim,
        step_raw,
        conv_inner,
        conv_group,
        bias_inner[None, :],
        bias_group,
        jnp.transpose(edge_inner, (1, 0, 2)),
        edge_group,
        jnp.reshape(init_states, (requests, inner, state)),
    )


PICKS = 16
PITCH = HALF + PICKS


def slot_ends(lengths, deal, first_row, shape, dim):
    requests = lengths.shape[0]
    slots = lax.broadcasted_iota(jnp.int32, shape, dim)
    ends = jnp.zeros(shape, jnp.int32)
    end = -1 - first_row
    for k in range(requests):
        end = end + lengths[k]
        ends = jnp.where(slots == deal[k], end, ends)
    return ends


def finish_kernel(
    lengths,
    deal,
    partial_y,
    mixed,
    decay_column,
    decay_row,
    step_row,
    reach_column,
    carry_column,
    state_own,
    gain_own,
    finals_own,
    factor_own,
    gate_in,
    inner_gain,
    w_out,
    tokens,
    w_head,
    final_gain,
    hidden,
    final_states,
    logits,
    weights,
    head,
    partials,
    stage_far,
    stage_near,
    land_far,
    land_near,
    stage_far2,
    stage_near2,
    land_far2,
    land_near2,
    picks,
    rows_all,
    wide_rows,
    load_sem,
    sends,
    recvs,
    pick_sends,
    pick_recvs,
    row_sends,
    row_recvs,
    outputs,
    normed,
    scales,
    entry_held,
    land_state,
    land_gain,
    square_own,
    square_land,
    outbox,
    pair_land,
    pair_sum,
    final_land,
    far_sends,
    far_recvs,
    row_stage,
    row_land,
    early_sends,
    early_recvs,
):
    rows, feat = tokens.shape
    heads, inner = decay_row.shape[0], gate_in.shape[1]
    size = inner // heads
    state = state_own.shape[1]
    requests = lengths.shape[0]
    seq = lax.axis_size("seq")
    load_out = pltpu.make_async_copy(w_out, weights, load_sem.at[0])
    load_head = pltpu.make_async_copy(w_head, head, load_sem.at[1])
    load_out.start()
    load_head.start()
    plane = [(dr, dc) for dr in range(4) for dc in range(4) if dr or dc]
    peers = [{axis: spot(axis, shift)} for axis, shift in PLANE]
    peers += [{"seq": spot("seq", shift)} for shift in range(1, seq)]
    peers += [
        {"row": spot("row", dr), "col": spot("col", dc)}
        for dr, dc in plane
        if not ((dr == 0 and dc != 2) or (dc == 0 and dr != 2))
    ]
    greet(peers)
    extra = []

    def hand(src, dst, number, place):
        copy = pltpu.make_async_remote_copy(
            src_ref=src,
            dst_ref=dst,
            send_sem=far_sends.at[number],
            recv_sem=far_recvs.at[number],
            device_id=place,
            device_id_type=MESH,
        )
        copy.start()
        extra.append(copy)
        return copy

    hand(state_own, land_state.at[0], 0, {"seq": spot("seq", 1)})
    hand(gain_own, land_gain, 1, {"seq": spot("seq", 1)})
    hand(state_own, land_state.at[1], 2, {"seq": spot("seq", 2)})

    def inside(b, carry):
        place = pl.ds(pl.multiple_of(b * BLOCK, BLOCK), BLOCK)
        scores = lax.dot_general(
            mixed[place, inner + state :],
            mixed[place, inner : inner + state],
            (((1,), (1,)), ((), ())),
            preferred_element_type=jnp.float32,
        )
        target = lax.broadcasted_iota(jnp.int32, (BLOCK, BLOCK), 0)
        source = lax.broadcasted_iota(jnp.int32, (BLOCK, BLOCK), 1)
        keep = (source <= target) & (source >= target - reach_column[place, :])
        for h in range(heads):
            span = slice(h * size, (h + 1) * size)
            diff = decay_column[place, h : h + 1] - decay_row[h : h + 1, place]
            decay = jnp.exp(jnp.where(keep, diff, NEVER))
            weight = (scores * decay * step_row[h : h + 1, place]).astype(jnp.bfloat16)
            outputs[place, span] = partial_y[place, span] + jnp.dot(
                weight, mixed[place, span], preferred_element_type=jnp.float32
            )
        return carry

    lax.fori_loop(0, rows // BLOCK, inside, 0)
    for copy in extra:
        copy.wait_recv()
    entry = land_state[0].astype(jnp.float32) + by_head(land_gain[...], size) * land_state[
        1
    ].astype(jnp.float32)
    entry_held[...] = entry
    carried = lax.dot_general(
        mixed[:, inner + state :],
        entry.astype(jnp.bfloat16),
        (((1,), (1,)), ((), ())),
        preferred_element_type=jnp.float32,
    )
    squares = jnp.zeros((rows, 128), jnp.float32)
    left = lax.broadcasted_iota(jnp.int32, (rows, 128), 1) < size
    for tile in range(inner // 128):
        span = slice(tile * 128, (tile + 1) * 128)
        coef = jnp.where(
            left, carry_column[:, 2 * tile : 2 * tile + 1], carry_column[:, 2 * tile + 1 : 2 * tile + 2]
        )
        gate = gate_in[:, span].astype(jnp.float32)
        gated = (outputs[:, span] + coef * carried[:, span]) * (gate / (1.0 + jnp.exp(-gate)))
        squares = squares + gated * gated
        value = (gated * inner_gain[:, span]).astype(jnp.bfloat16)
        normed[0:HALF, span] = value[0:HALF]
        normed[PITCH : PITCH + HALF, span] = value[HALF:]
    square_own[...] = jnp.broadcast_to(
        jnp.sum(squares.T, axis=0, keepdims=True), square_own.shape
    )
    partner = lax.axis_index("col") + 1 - 2 * lax.rem(lax.axis_index("col"), 2)
    square_copy = hand(square_own, square_land, 3, {"col": partner})
    ends = slot_ends(lengths, deal, lax.axis_index("seq") * rows, (requests, rows), 0)
    chosen = ends == lax.broadcasted_iota(jnp.int32, (requests, rows), 1)
    chooser = chosen.astype(jnp.float32).astype(jnp.bfloat16)
    picked = jnp.dot(chooser[:, :HALF], normed[0:HALF, :], preferred_element_type=jnp.float32)
    picked = picked + jnp.dot(
        chooser[:, HALF:], normed[PITCH : PITCH + HALF, :], preferred_element_type=jnp.float32
    )
    for half in (0, 1):
        normed[half * PITCH + HALF : half * PITCH + PITCH, :] = picked.astype(jnp.bfloat16)
    load_out.wait()

    def compute(first, count, scale=None):
        def body(i, carry):
            half = lax.rem(i, 2)
            j = i // 2 + first
            dv = 2 - j // 4 - j // 8 + (j // 12) * 2
            du = 2 - lax.rem(j, 4) - lax.rem(j, 4) // 2 + (lax.rem(j, 4) // 3) * 2
            block = block_of(half, du, dv)
            place = pl.ds(pl.multiple_of(half * PITCH, PICKS), PITCH)
            value = jnp.dot(
                normed[place, :],
                weights[:, pl.ds(pl.multiple_of(block * feat, feat), feat)],
                preferred_element_type=jnp.float32,
            )
            if scale is not None:
                value = value * scale[place, :]
            partials[half, j] = value
            return carry

        lax.fori_loop(0, 2 * count, body, 0)

    started = {}

    def send(half, number, src, dst, axis, shift):
        copy = remote(src, dst, sends.at[half], recvs.at[half], number, axis, shift)
        copy.start()
        started[half, number] = copy

    def far(half, values, stage, land, number, axis):
        for side in (0, 1):
            stage[side] = values[side * 128 : side * 128 + 128].astype(jnp.bfloat16)
            send(half, number + side, stage.at[side], land.at[side], axis, 1 - 2 * side)

    def near(half, side, values, far_land, far_number, stage, land, number, axis):
        started[half, far_number + side].wait_recv()
        extra = far_land[side].astype(jnp.float32)
        keep = slice(128 - 128 * side, 256 - 128 * side)
        mix = slice(128 * side, 128 * side + 128)
        stage[side, mix] = (values[mix] + extra).astype(jnp.bfloat16)
        stage[side, keep] = values[keep].astype(jnp.bfloat16)
        send(half, number + side, stage.at[side], land.at[side], axis, 1 - 2 * side)

    compute(0, 4)
    square_copy.wait_recv()
    both = square_own[0:1, :] + square_land[0:1, :]
    scale_row = lax.rsqrt(both / (2 * inner) + EPSILON)
    scale_tile = jnp.broadcast_to(scale_row, (128, rows)).T
    wide_scale = jnp.concatenate([scale_tile, scale_tile], axis=1)
    pick_scale = jnp.broadcast_to(
        jnp.sum(jnp.where(chosen, scale_row, 0.0), axis=1, keepdims=True), (requests, feat)
    )
    for half in (0, 1):
        start = half * PITCH
        scales[start : start + HALF, :] = wide_scale[half * HALF : half * HALF + HALF]
        scales[start + HALF : start + PITCH, :] = pick_scale
    for k in range(4):
        for half in (0, 1):
            far(
                half,
                partials[half, k, 0:HALF] * scales[half * PITCH : half * PITCH + HALF, :],
                stage_far.at[half, k],
                land_far.at[half, k],
                2 * k,
                AXES[half][1],
            )
    compute(4, 12, scales)
    row_copies = []
    for j in range(15):
        dv, du = (2, 1, -1, 0)[j // 4], (2, 1, -1, 0)[j % 4]
        value = partials[0, j, HALF:PITCH]
        if j < 4:
            value = value * pick_scale
        row_stage[j] = value.astype(jnp.bfloat16)
        copy = pltpu.make_async_remote_copy(
            src_ref=row_stage.at[j],
            dst_ref=row_land.at[j],
            send_sem=early_sends.at[j],
            recv_sem=early_recvs.at[j],
            device_id={"row": spot("row", dv), "col": spot("col", du)},
            device_id_type=MESH,
        )
        copy.start()
        row_copies.append(copy)
    core = lax.rem(lax.axis_index("seq"), 2)
    chip = lax.axis_index("seq") // 2
    chips = seq // 2

    for k in range(4):
        for half in (0, 1):
            for side in (0, 1):
                near(
                    half,
                    side,
                    partials[half, 4 + 4 * side + k, 0:HALF],
                    land_far.at[half, k],
                    2 * k,
                    stage_near.at[half, k],
                    land_near.at[half, k],
                    8 + 2 * k,
                    AXES[half][1],
                )
    def fill(o, carry):
        value = finals_own[o].astype(jnp.float32) + by_head(factor_own[o], size) * entry_held[...]
        outbox[lax.rem(o // 2, 2), o // 4, lax.rem(o, 2)] = value.astype(jnp.bfloat16)
        return carry

    lax.fori_loop(0, requests, fill, 0)
    pair_copy = hand(outbox.at[1 - core], pair_land, 4, {"seq": spot("seq", 1 - 2 * core)})
    row_total = partials[0, 15, HALF:PITCH]
    row_total = row_total + jnp.dot(chooser, tokens[...], preferred_element_type=jnp.float32)
    for j, copy in enumerate(row_copies):
        copy.wait_recv()
        row_total = row_total + row_land[j].astype(jnp.float32)
    picks[0] = row_total.astype(jnp.bfloat16)
    handed = []
    for shift in range(1, seq):
        copy = remote(
            picks.at[0], picks.at[shift], pick_sends, pick_recvs, shift, "seq", shift
        )
        copy.start()
        handed.append(copy)
    own = block_of(0, 0, 0)

    def gather_rows():
        for copy in handed[: seq - 1]:
            copy.wait_recv()
        whole = picks[0].astype(jnp.float32)
        for shift in range(1, seq):
            whole = whole + picks[shift].astype(jnp.float32)
        rows_all[own] = whole.astype(jnp.bfloat16)
        for number, (dr, dc) in enumerate(plane):
            copy = pltpu.make_async_remote_copy(
                src_ref=rows_all.at[own],
                dst_ref=rows_all.at[own],
                send_sem=row_sends.at[number],
                recv_sem=row_recvs.at[number],
                device_id={"row": spot("row", dr), "col": spot("col", dc)},
                device_id_type=MESH,
            )
            copy.start()
            handed.append(copy)

    pair_copy.wait_recv()
    for d in range(chips):
        there = lax.rem(chip + d, chips)
        pair_sum[d] = (
            outbox[core, there].astype(jnp.float32) + pair_land[there].astype(jnp.float32)
        ).astype(jnp.bfloat16)
    final_copies = [
        hand(pair_sum.at[d], final_land.at[d - 1], 4 + d, {"seq": spot("seq", 2 * d)})
        for d in range(1, chips)
    ]
    for k in range(4):
        if k == 2:
            gather_rows()
        for half in (0, 1):
            axis = AXES[half][0]
            total = partials[half, 12 + k, 0:HALF]
            for side in (0, 1):
                started[half, 8 + 2 * k + side].wait_recv()
                total = total + land_near[half, k, side].astype(jnp.float32)
            if k == 0:
                far(half, total, stage_far2.at[half], land_far2.at[half], 16, axis)
            elif k < 3:
                near(
                    half,
                    k - 1,
                    total,
                    land_far2.at[half],
                    16,
                    stage_near2.at[half],
                    land_near2.at[half],
                    18,
                    axis,
                )
            else:
                for side in (0, 1):
                    started[half, 18 + side].wait_recv()
                    total = total + land_near2[half, side].astype(jnp.float32)
                place = slice(half * HALF, half * HALF + HALF)
                hidden[place, :] = (tokens[place, :].astype(jnp.float32) + total).astype(
                    jnp.bfloat16
                )
    for copy in handed[seq - 1 :]:
        copy.wait_recv()
    for copy in final_copies:
        copy.wait_recv()
    final = pair_sum[0].astype(jnp.float32)
    for d in range(1, chips):
        final = final + final_land[d - 1].astype(jnp.float32)
    final_states[...] = final
    load_head.wait()
    total = jnp.zeros((requests, 128), jnp.float32)
    for block in range(len(plane) + 1):
        value = rows_all[block].astype(jnp.float32)
        wide_rows[:, block * feat : (block + 1) * feat] = value
        total = total + value[:, :128] * value[:, :128] + value[:, 128:] * value[:, 128:]
    depth = w_head.shape[0]
    scale = lax.rsqrt(jnp.sum(total, axis=1, keepdims=True) / depth + EPSILON)
    head_in = (wide_rows[...] * scale * final_gain[...]).astype(jnp.bfloat16)
    logits[...] = jnp.dot(head_in, head[...], preferred_element_type=jnp.float32)
    for copy in handed:
        copy.wait_send()
    for copy in list(started.values()) + extra + row_copies:
        copy.wait_send()


def finish(lengths, deal, arrays, gate_in, inner_gain, w_out, tokens, w_head, final_gain):
    rows, feat = tokens.shape
    inner, depth = w_out.shape
    requests = lengths.shape[0]
    vocab = w_head.shape[1]
    seq = lax.axis_size("seq")
    state = arrays[7].shape[1]
    heads = arrays[8].shape[0]
    slots = requests // seq
    smem = pl.BlockSpec(memory_space=pltpu.SMEM)
    vmem = pl.BlockSpec(memory_space=pltpu.VMEM)
    anywhere = pl.BlockSpec(memory_space=pl.ANY)
    bf, f32 = jnp.bfloat16, jnp.float32
    return pl.pallas_call(
        finish_kernel,
        out_shape=[
            jax.ShapeDtypeStruct((rows, feat), bf),
            jax.ShapeDtypeStruct((slots, inner, state), f32),
            jax.ShapeDtypeStruct((requests, vocab), f32),
        ],
        in_specs=[smem, smem] + [vmem] * 13 + [anywhere, vmem, anywhere, vmem],
        out_specs=[vmem] * 3,
        scratch_shapes=[
            pltpu.VMEM((inner, depth), bf),
            pltpu.VMEM((depth, vocab), bf),
            pltpu.VMEM((2, 16, PITCH, feat), f32),
            pltpu.VMEM((2, 4, 2, 128, feat), bf),
            pltpu.VMEM((2, 4, 2, 256, feat), bf),
            pltpu.VMEM((2, 4, 2, 128, feat), bf),
            pltpu.VMEM((2, 4, 2, 256, feat), bf),
            pltpu.VMEM((2, 2, 128, feat), bf),
            pltpu.VMEM((2, 2, 256, feat), bf),
            pltpu.VMEM((2, 2, 128, feat), bf),
            pltpu.VMEM((2, 2, 256, feat), bf),
            pltpu.VMEM((seq, requests, feat), bf),
            pltpu.VMEM((16, requests, feat), bf),
            pltpu.VMEM((requests, depth), f32),
            pltpu.SemaphoreType.DMA((2,)),
            pltpu.SemaphoreType.DMA((2, 20)),
            pltpu.SemaphoreType.DMA((2, 20)),
            pltpu.SemaphoreType.DMA((seq,)),
            pltpu.SemaphoreType.DMA((seq,)),
            pltpu.SemaphoreType.DMA((15,)),
            pltpu.SemaphoreType.DMA((15,)),
            pltpu.VMEM((rows, inner), f32),
            pltpu.VMEM((2 * PITCH, inner), bf),
            pltpu.VMEM((2 * PITCH, feat), f32),
            pltpu.VMEM((inner, state), f32),
            pltpu.VMEM((2, inner, state), bf),
            pltpu.VMEM((heads, state), f32),
            pltpu.VMEM((8, rows), f32),
            pltpu.VMEM((8, rows), f32),
            pltpu.VMEM((2, seq // 2, slots, inner, state), bf),
            pltpu.VMEM((seq // 2, slots, inner, state), bf),
            pltpu.VMEM((seq // 2, slots, inner, state), bf),
            pltpu.VMEM((seq // 2 - 1, slots, inner, state), bf),
            pltpu.SemaphoreType.DMA((8,)),
            pltpu.SemaphoreType.DMA((8,)),
            pltpu.VMEM((15, requests, feat), bf),
            pltpu.VMEM((15, requests, feat), bf),
            pltpu.SemaphoreType.DMA((15,)),
            pltpu.SemaphoreType.DMA((15,)),
        ],
        compiler_params=pltpu.CompilerParams(
            collective_id=1, has_side_effects=True, vmem_limit_bytes=VMEM_LIMIT
        ),
        name="finish",
    )(
        lengths,
        deal,
        *arrays,
        gate_in,
        inner_gain[None, :],
        w_out,
        tokens,
        w_head,
        final_gain[None, :],
    )


def deliver_kernel(*refs):
    count = len(refs) // 2
    sems = refs[-1]
    copies = [
        pltpu.make_async_copy(refs[i], refs[count + i], sems.at[i]) for i in range(count)
    ]
    for copy in copies:
        copy.start()
    for copy in copies:
        copy.wait()


def deliver(*arrays):
    return pl.pallas_call(
        deliver_kernel,
        out_shape=[jax.ShapeDtypeStruct(a.shape, a.dtype) for a in arrays],
        in_specs=[pl.BlockSpec(memory_space=pltpu.VMEM)] * len(arrays),
        out_specs=[pl.BlockSpec(memory_space=pl.ANY)] * len(arrays),
        scratch_shapes=[pltpu.SemaphoreType.DMA((len(arrays),))],
        name="deliver",
    )(*arrays)


def per_device(
    tokens,
    lengths,
    deal,
    pre_gain,
    w_inner,
    w_group,
    w_step,
    conv_inner,
    conv_group,
    conv_bias_inner,
    conv_bias_group,
    edge_inner,
    edge_group,
    init_states,
    step_bias,
    decay_log,
    skip,
    inner_gain,
    w_out,
    final_gain,
    w_head,
):
    inner = conv_inner.shape[1]
    state = w_group.shape[3]
    heads = w_step.shape[1]
    gate_in, chan, step_raw, rim = project(tokens, w_inner, w_group, w_step, pre_gain)
    arrays = scan(
        lengths,
        deal,
        step_bias,
        decay_log,
        skip,
        chan,
        rim,
        step_raw,
        conv_inner,
        conv_group,
        conv_bias_inner,
        conv_bias_group,
        edge_inner,
        edge_group,
        init_states,
    )
    hidden_out, final_states, logits = finish(
        lengths, deal, arrays, gate_in, inner_gain, w_out, tokens, w_head, final_gain
    )
    hidden_out, final_states, logits = deliver(hidden_out, final_states, logits)
    final_states = jnp.reshape(
        final_states, (final_states.shape[0], heads, inner // heads, state)
    )
    return (hidden_out, final_states, logits)


def solution(mesh):
    in_specs = (
        P("seq", ("row", "col")),
        P(),
        P(),
        P(),
        P(None, None, ("row", "col")),
        P(None, None, "row", None),
        P(None, ("row", "col")),
        P(None, ("row", "col")),
        P(None, None, "row", None),
        P(("row", "col")),
        P(None, "row", None),
        P(None, None, ("row", "col")),
        P(None, None, None, "row", None),
        P(None, ("row", "col"), None, None),
        P(("row", "col")),
        P(("row", "col")),
        P(("row", "col")),
        P(("row", "col")),
        P(("row", "col"), None),
        P(),
        P(None, ("seq", "row", "col")),
    )
    out_specs = (
        P("seq", ("row", "col")),
        P("seq", ("row", "col"), None, None),
        P(None, ("seq", "row", "col")),
    )
    return jax.shard_map(
        per_device, mesh=mesh, in_specs=in_specs, out_specs=out_specs, check_vma=False
    )
```
